256 devices in a mesh: seq: 64 (over x_hi, y, z), doc: 4 (over x_lo, core).
Axes of the slice: x: 4 (x_hi: 2, x_lo: 2; x = x_hi * 2 + x_lo), y: 4, z: 8, core: 2. Of those that a mesh axis runs over, the one named last changes fastest.
Arguments:
- tokens: bfloat16 [4, 8192, 4096], P('doc', 'seq'), may hold values from -6 to 6
- norm_gain: float32 [4096], replicated, may hold values from 0.5 to 9
- w_query: bfloat16 [4096, 2048], P(None, 'doc'), may hold values from -0.09375 to 0.09375
- key_weight: bfloat16 [4096, 512], P(None, 'doc'), may hold values from -0.09375 to 0.09375
- value_weight: bfloat16 [4096, 512], P(None, 'doc'), may hold values from -0.09375 to 0.09375
- vertical_blocks: int32 [4, 4, 4], replicated, may hold values from 0 to 63, as said below
- slash_offsets: int32 [4, 4, 4], replicated, may hold values from 2 to 63, as said below
Outputs:
- attended: bfloat16 [4, 8192, 2048], P('doc', 'seq')
The draws below stay inside these ranges and needn't reach their ends.
Inputs may be any that keep to these rules, and one draw needn't show every extreme that they name: `vertical_blocks`: within one document and key-value head the 4 block indices are distinct. `slash_offsets`: within one document and key-value head the 4 offsets are distinct.
All inputs are finite; a program needn't handle non-finite values.
Results may differ from the reference program's by a relative error of at most 0.013.
The reference program's roundings to bfloat16 on the way count: a program that leaves them out, or rounds other values in their place, can miss the bound.
Values may be sent and summed in bfloat16 or wider, within the bound.
A program may use at most 64 MiB of HBM per device.

```python
import jax
import jax.numpy as jnp
from jax import lax

MODEL_WIDTH = 4096
QUERY_HEADS = 16
KEY_VALUE_HEADS = 4
HEAD_WIDTH = 128
BLOCK_TOKENS = 128
VERTICAL_TOTAL = 4
SLASH_TOTAL = 4
DOCUMENT_COUNT = 4
LEN = 8192


def unique_rows(key, rows, width, low, high):
    span = high - low
    row_keys = jax.random.split(key, rows)
    common = jax.vmap(lambda row_key: jax.random.permutation(row_key, span)[:width])(row_keys) + low
    top_row = jnp.concatenate([jax.random.permutation(row_keys[0], span - 1)[:width - 1] + low, jnp.full((1,), high - 1, jnp.int32)])
    bottom_row = jnp.concatenate([jax.random.permutation(row_keys[1], span - 1)[:width - 1] + low + 1, jnp.full((1,), low, jnp.int32)])
    return common.astype(jnp.int32).at[0].set(top_row.astype(jnp.int32)).at[1].set(bottom_row.astype(jnp.int32))


def draw_vertical_blocks(key, part):
    block_list = LEN // BLOCK_TOKENS
    return unique_rows(jax.random.fold_in(key, 11), DOCUMENT_COUNT * KEY_VALUE_HEADS, VERTICAL_TOTAL, 0, block_list).reshape(DOCUMENT_COUNT, KEY_VALUE_HEADS, VERTICAL_TOTAL)


def draw_slash_offsets(key, part):
    block_list = LEN // BLOCK_TOKENS
    return unique_rows(jax.random.fold_in(key, 23), DOCUMENT_COUNT * KEY_VALUE_HEADS, SLASH_TOTAL, 2, block_list).reshape(DOCUMENT_COUNT, KEY_VALUE_HEADS, SLASH_TOTAL)


def draw_norm_gain(key, part):
    value_rows = jax.random.uniform(key, (MODEL_WIDTH,), jnp.float32, 0.5, 1.5)
    return value_rows


def block_levels(own_key, shape, cuts, smallest, high):
    loudness, own = 1.0, jax.random.fold_in(own_key, 6)
    for dim, shards_of in cuts:
        steps = jnp.exp(jax.random.uniform(jax.random.fold_in(own, dim), (shards_of,), jnp.float32, smallest / len(cuts), high / len(cuts)))
        loudness = loudness * jnp.repeat(steps, shape[dim] // shards_of).reshape([-1 if axis == dim else 1 for axis in range(len(shape))])
    return loudness


def bell_draw(stream_key, shape, deviation, reach, shards=(), held_as=jnp.bfloat16):
    level = block_levels(stream_key, shape, shards, -0.22, 0.18) if shards else 1.0
    array = jax.random.normal(stream_key, shape, jnp.float32) * deviation * level
    return jnp.minimum(jnp.maximum(array, -reach), reach).astype(held_as)


def setup_inputs(seed: int = 0) -> dict:
    streams_of = jax.random.split(jax.random.key(seed), 8)
    return {
        "tokens": bell_draw(streams_of[0], (DOCUMENT_COUNT, LEN, MODEL_WIDTH), 1.0, 6.0, ((0, 4), (1, 64))),
        "norm_gain": draw_norm_gain(jax.random.fold_in(streams_of[7], 71), 0),
        "w_query": bell_draw(streams_of[2], (MODEL_WIDTH, QUERY_HEADS * HEAD_WIDTH), MODEL_WIDTH ** -0.5, 0.09375, ((1, 4),)),
        "key_weight": bell_draw(streams_of[3], (MODEL_WIDTH, KEY_VALUE_HEADS * HEAD_WIDTH), MODEL_WIDTH ** -0.5, 0.09375, ((1, 4),)),
        "value_weight": bell_draw(streams_of[4], (MODEL_WIDTH, KEY_VALUE_HEADS * HEAD_WIDTH), MODEL_WIDTH ** -0.5, 0.09375, ((1, 4),)),
        "vertical_blocks": draw_vertical_blocks(jax.random.fold_in(streams_of[7], 71), 0),
        "slash_offsets": draw_slash_offsets(jax.random.fold_in(streams_of[7], 71), 0),
    }


def rope_table(positions, width):
    inverse = jnp.power(jnp.float32(500000.0), -jnp.arange(0, width, 2, dtype=jnp.float32) / width)
    angles = positions.astype(jnp.float32)[:, None] * inverse[None, :]
    return (jnp.cos(angles), jnp.sin(angles))

def apply_rotation(value_rows, cosine_table, sine_table):
    half = value_rows.shape[-1] // 2
    first = value_rows[..., :half]
    second = value_rows[..., half:]
    cosine_table = cosine_table[:, None, :]
    sine_table = sine_table[:, None, :]
    return jnp.concatenate([first * cosine_table - second * sine_table, second * cosine_table + first * sine_table], axis=-1)

def normalize(tokens, norm_gain):
    widened = tokens.astype(jnp.float32)
    scale = lax.rsqrt(lax.optimization_barrier(jnp.mean(widened * widened, axis=-1, keepdims=True)) + 1e-05)
    return (widened * scale * norm_gain).astype(jnp.bfloat16)

def slot_masks(rows, slots):
    query_index = jnp.arange(rows)[:, None, None]
    key_index = jnp.arange(rows)[None, None, :]
    slot_index = jnp.arange(slots)[None, :, None]
    return (slot_index > 0) | (key_index <= query_index)

def block_validity(place, vertical, offsets):
    slash_index = place - offsets
    repeated = jnp.any(vertical[..., :, None] == slash_index[..., None, :], axis=-1)
    own = jnp.ones(slash_index.shape[:-1] + (1,), dtype=jnp.bool_)
    previous = jnp.broadcast_to(place >= 1, own.shape)
    return jnp.concatenate([own, previous, slash_index >= 0, (vertical < place - 1) & ~repeated], axis=-1)

def reference(tokens, norm_gain, w_query, key_weight, value_weight, vertical_blocks, slash_offsets):
    document_list, sequence_length, width = tokens.shape
    query_group = QUERY_HEADS // KEY_VALUE_HEADS
    block_list = sequence_length // BLOCK_TOKENS
    normed_input = normalize(tokens, norm_gain).reshape(document_list * sequence_length, width)
    cosine_table, sine_table = rope_table(jnp.arange(sequence_length, dtype=jnp.int32), HEAD_WIDTH)
    query_rows = jnp.dot(normed_input, w_query, preferred_element_type=jnp.float32).reshape(document_list, sequence_length, QUERY_HEADS, HEAD_WIDTH)
    query_rows = apply_rotation(query_rows, cosine_table, sine_table).astype(jnp.bfloat16).reshape(document_list, sequence_length, KEY_VALUE_HEADS, query_group, HEAD_WIDTH)
    key_rows = jnp.dot(normed_input, key_weight, preferred_element_type=jnp.float32).reshape(document_list, sequence_length, KEY_VALUE_HEADS, HEAD_WIDTH)
    key_rows = apply_rotation(key_rows, cosine_table, sine_table).astype(jnp.bfloat16)
    value_rows = jnp.dot(normed_input, value_weight, preferred_element_type=jnp.float32).reshape(document_list, sequence_length, KEY_VALUE_HEADS, HEAD_WIDTH).astype(jnp.bfloat16)
    query_streams = jnp.transpose(query_rows, (0, 2, 1, 3, 4)).reshape(document_list * KEY_VALUE_HEADS, block_list, BLOCK_TOKENS, query_group, HEAD_WIDTH)
    key_streams = jnp.transpose(key_rows, (0, 2, 1, 3)).reshape(document_list * KEY_VALUE_HEADS, block_list, BLOCK_TOKENS, HEAD_WIDTH)
    value_streams = jnp.transpose(value_rows, (0, 2, 1, 3)).reshape(document_list * KEY_VALUE_HEADS, block_list, BLOCK_TOKENS, HEAD_WIDTH)
    masks = slot_masks(BLOCK_TOKENS, 2 + SLASH_TOTAL + VERTICAL_TOTAL)
    index = jnp.arange(block_list, dtype=jnp.int32)[:, None]

    def one_lane(items):
        query_lane, key_lane, value_lane, vertical, offsets = items
        chosen = jnp.concatenate([index, index - 1, index - offsets[None, :], jnp.broadcast_to(vertical[None, :], (block_list, vertical.shape[0]))], axis=1)
        chosen = jnp.clip(chosen, 0, block_list - 1).astype(jnp.int32)
        valid = block_validity(index, vertical, offsets)
        key_blocks = key_lane[chosen]
        value_blocks = value_lane[chosen]
        scores = jnp.einsum('bqgd,bskd->bgqsk', query_lane.astype(jnp.float32), key_blocks.astype(jnp.float32)) * HEAD_WIDTH ** (-0.5)
        mask = valid[:, None, None, :, None] & masks[None, None]
        scores = jnp.where(mask, scores, -jnp.inf)
        highest = lax.optimization_barrier(jnp.max(scores, axis=(3, 4), keepdims=True))
        raised = jnp.exp(scores - highest)
        total = lax.optimization_barrier(jnp.sum(raised, axis=(3, 4)))
        weights = raised.astype(jnp.bfloat16)
        mixed_output = jnp.einsum('bgqsk,bskd->bqgd', weights.astype(jnp.float32), value_blocks.astype(jnp.float32))
        mixed_output = mixed_output / jnp.transpose(total, (0, 2, 1))[..., None]
        return mixed_output.astype(jnp.bfloat16).reshape(sequence_length, query_group * HEAD_WIDTH)
    mixed_output = lax.map(one_lane, (query_streams, key_streams, value_streams, vertical_blocks.reshape(-1, VERTICAL_TOTAL), slash_offsets.reshape(-1, SLASH_TOTAL)))
    return jnp.transpose(mixed_output.reshape(document_list, KEY_VALUE_HEADS, sequence_length, query_group * HEAD_WIDTH), (0, 2, 1, 3)).reshape(document_list, sequence_length, QUERY_HEADS * HEAD_WIDTH)
```

```python
import jax
import jax.numpy as jnp
from jax import lax
from jax.sharding import PartitionSpec as P

QUERY_HEADS = 16
KEY_VALUE_HEADS = 4
HEAD_WIDTH = 128


def rope_table(positions, width):
    inverse = jnp.power(jnp.float32(500000.0), -jnp.arange(0, width, 2, dtype=jnp.float32) / width)
    angles = positions.astype(jnp.float32)[:, None] * inverse[None, :]
    return (jnp.cos(angles), jnp.sin(angles))


def apply_rotation(value_rows, cosine_table, sine_table):
    half = value_rows.shape[-1] // 2
    first = value_rows[..., :half]
    second = value_rows[..., half:]
    cosine_table = cosine_table[:, None, :]
    sine_table = sine_table[:, None, :]
    return jnp.concatenate(
        [first * cosine_table - second * sine_table, second * cosine_table + first * sine_table],
        axis=-1,
    )


def normalize(tokens, norm_gain):
    widened = tokens.astype(jnp.float32)
    scale = lax.rsqrt(jnp.mean(widened * widened, axis=-1, keepdims=True) + 1e-05)
    return (widened * scale * norm_gain).astype(jnp.bfloat16)


def slot_masks(rows, slots):
    query_index = jnp.arange(rows)[:, None, None]
    key_index = jnp.arange(rows)[None, None, :]
    slot_index = jnp.arange(slots)[None, :, None]
    return (slot_index > 0) | (key_index <= query_index)


def block_validity(place, vertical, offsets):
    slash_index = place - offsets
    repeated = jnp.any(vertical[..., :, None] == slash_index[..., None, :], axis=-1)
    own = jnp.ones(slash_index.shape[:-1] + (1,), dtype=jnp.bool_)
    previous = jnp.broadcast_to(place >= 1, own.shape)
    return jnp.concatenate(
        [own, previous, slash_index >= 0, (vertical < place - 1) & ~repeated], axis=-1
    )


def attend(query_rows, keys_all, valid, masks):
    width = query_rows.shape[-1]
    scores = jnp.einsum(
        "lqhgd,lskhd->lhgqsk", query_rows, keys_all[..., :width], preferred_element_type=jnp.float32
    ) * width ** (-0.5)
    mask = valid[:, :, None, None, :, None] & masks[None, None, None]
    scores = jnp.where(mask, scores, -jnp.inf)
    highest = jnp.max(scores, axis=(4, 5), keepdims=True)
    raised = jnp.exp(scores - highest)
    total = jnp.sum(raised, axis=(4, 5))
    weights = raised.astype(jnp.bfloat16)
    mixed_output = jnp.einsum(
        "lhgqsk,lskhd->lqhgd", weights, keys_all[..., width:], preferred_element_type=jnp.float32
    )
    mixed_output = mixed_output / jnp.transpose(total, (0, 3, 1, 2))[..., None]
    return mixed_output.astype(jnp.bfloat16).reshape(query_rows.shape[0], query_rows.shape[1], -1)


def local(tokens, norm_gain, w_query, key_weight, value_weight, vertical_blocks, slash_offsets):
    local_docs, rows, width = tokens.shape
    query_group = QUERY_HEADS // KEY_VALUE_HEADS
    place = lax.axis_index("seq")
    doc_place = lax.axis_index("doc")
    normed_input = normalize(tokens, norm_gain)
    cosine_table, sine_table = rope_table(
        place * rows + jnp.arange(rows, dtype=jnp.int32), HEAD_WIDTH
    )
    local_heads = key_weight.shape[1] // HEAD_WIDTH
    query_cols = local_heads * query_group * HEAD_WIDTH
    piece = lax.all_gather(normed_input, "doc", axis=0, tiled=True)
    amount = piece.shape[0]
    flat = piece.reshape(amount * rows, width)
    query_part = jnp.dot(flat, w_query, preferred_element_type=jnp.float32).reshape(
        amount, rows, local_heads * query_group, HEAD_WIDTH
    )
    key_part = jnp.dot(flat, key_weight, preferred_element_type=jnp.float32).reshape(
        amount, rows, local_heads, HEAD_WIDTH
    )
    value_part = jnp.dot(flat, value_weight, preferred_element_type=jnp.float32).reshape(
        amount, rows, local_heads, HEAD_WIDTH
    )
    query_part = (
        apply_rotation(query_part, cosine_table, sine_table)
        .astype(jnp.bfloat16)
        .reshape(amount, rows, query_cols)
    )
    joined = jnp.concatenate(
        [
            apply_rotation(key_part, cosine_table, sine_table).astype(jnp.bfloat16),
            value_part.astype(jnp.bfloat16),
        ],
        axis=-1,
    )
    projected = jnp.concatenate(
        [query_part, joined.reshape(amount, rows, local_heads * 2 * HEAD_WIDTH)], axis=-1
    )
    lanes = projected.shape[0]
    query_rows = projected[:, :, :query_cols].reshape(
        lanes, rows, local_heads, query_group, HEAD_WIDTH
    )
    key_value = projected[:, :, query_cols:].reshape(lanes, rows, local_heads, 2 * HEAD_WIDTH)
    vertical = lax.dynamic_slice_in_dim(vertical_blocks, doc_place * local_heads, local_heads, 1)
    offsets = lax.dynamic_slice_in_dim(slash_offsets, doc_place * local_heads, local_heads, 1)
    lanes = key_value.shape[0]
    gathered = lax.all_gather(key_value[:, :, 0], "seq", axis=0)
    near = jnp.broadcast_to(jnp.stack([place, place - 1]), (lanes, 2))
    chosen = jnp.concatenate([near, place - offsets[:, 0], vertical[:, 0]], axis=1)
    chosen = jnp.clip(chosen, 0, gathered.shape[0] - 1)
    keys_all = gathered[chosen, jnp.arange(lanes)[:, None]][:, :, :, None]
    valid = block_validity(place, vertical, offsets)
    mixed_output = attend(query_rows, keys_all, valid, slot_masks(rows, keys_all.shape[1]))
    return lax.all_to_all(mixed_output, "doc", split_axis=0, concat_axis=2, tiled=True)


def solution(mesh):
    return jax.shard_map(
        local,
        mesh=mesh,
        in_specs=(
            P("doc", "seq", None),
            P(),
            P(None, "doc"),
            P(None, "doc"),
            P(None, "doc"),
            P(),
            P(),
        ),
        out_specs=P("doc", "seq", None),
        check_vma=False,
    )
```

```python
import functools

import jax
import jax.numpy as jnp
from jax import lax
from jax.experimental import pallas as pl
from jax.experimental.pallas import tpu as pltpu
from jax.sharding import PartitionSpec as P

MESH = pl.DeviceIdType.MESH
HEADS = 4
HW = 128
ROWS = 128
WIDTH = 4096
DOCS = 4
RING = 8
COLS = 4
SLOTS = 4
CHUNKS = 4
LINE = 64


def rope_tables(place):
    positions = place * ROWS + jnp.arange(ROWS, dtype=jnp.int32)
    inverse = jnp.power(jnp.float32(500000.0), -jnp.arange(0, HW, 2, dtype=jnp.float32) / HW)
    angles = positions.astype(jnp.float32)[:, None] * inverse[None, :]
    cosine, sine = jnp.cos(angles), jnp.sin(angles)
    return jnp.concatenate([cosine, cosine], axis=1), jnp.concatenate([-sine, sine], axis=1)


def take(refs, *counts):
    refs = list(refs)
    out = []
    for count in counts:
        out.append(refs[:count] if count > 1 else refs[0])
        del refs[:count]
    return out


def kernel(vert_ref, slash_ref, tok_hbm, gain_ref, wq_hbm, wk_hbm, wv_hbm, cos_ref, sin_ref, out_hbm, *scratch):
    (
        tok, normed, w, kv, prev, ya, yb, xc, vy, vx, vz, qb, kall, vall, ob,
        local_sem, t_send, t_recv, f_send, f_recv, p_send, p_recv, z_send, z_recv, y_send, y_recv,
        x_send, x_recv, vy_send, vy_recv, vx_send, vx_recv, vz_send, vz_recv, o_send, o_recv,
    ) = take(
        scratch, 4, 4, 1, 4, 4, 4, 4, 4, 4, 4, 4, 4, 1, 1, 4, *([1] * 21)
    )
    s = lax.axis_index("seq")
    g = lax.axis_index("doc")
    z = lax.rem(s, RING)
    row = s // RING
    y = lax.rem(row, COLS)
    x = row // COLS
    docs = [g, g + 1 - 2 * lax.rem(g, 2), lax.rem(g + 2, 4), 3 - g]

    def at(seq, doc):
        return {"seq": seq, "doc": doc}

    z_up = at(s - z + lax.rem(z + 1, RING), g)
    z_down = at(s - z + lax.rem(z + RING - 1, RING), g)
    y_up = at(s - y * RING + lax.rem(y + 1, COLS) * RING, g)
    y_far = at(s - y * RING + lax.rem(y + 2, COLS) * RING, g)
    y_down = at(s - y * RING + lax.rem(y + 3, COLS) * RING, g)
    x_far = at(lax.rem(s + LINE // 2, LINE), g)
    after = at(lax.rem(s + 1, LINE), g)
    before = at(lax.rem(s + LINE - 1, LINE), g)
    mates = [None] + [at(s, docs[k]) for k in range(1, 4)]

    def remote(src, dst, send, recv, device):
        return pltpu.make_async_remote_copy(
            src_ref=src, dst_ref=dst, send_sem=send, recv_sem=recv, device_id=device, device_id_type=MESH
        )

    loads = [
        pltpu.make_async_copy(tok_hbm, tok[0], local_sem.at[0]),
        pltpu.make_async_copy(wk_hbm, w.at[:, 0:HW], local_sem.at[1]),
        pltpu.make_async_copy(wv_hbm, w.at[:, HW : 2 * HW], local_sem.at[2]),
        pltpu.make_async_copy(wq_hbm, w.at[:, 2 * HW :], local_sem.at[3]),
    ]
    for load in loads:
        load.start()

    barrier = pltpu.get_barrier_semaphore()
    greeted = mates[1:] + [z_up, z_down, y_up, y_far, y_down, x_far, after, before]
    for device in greeted:
        pl.semaphore_signal(barrier, inc=1, device_id=device, device_id_type=MESH)
    pl.semaphore_wait(barrier, len(greeted))

    part = ROWS // CHUNKS

    def rows_of(c):
        return pl.ds(c * part, part)

    across = [
        remote(tok_hbm.at[rows_of(c)], tok[2].at[rows_of(c)], t_send.at[c], t_recv.at[c], mates[2])
        for c in range(CHUNKS)
    ]
    beside = remote(tok_hbm, tok[1], t_send.at[CHUNKS], t_recv.at[CHUNKS], mates[1])
    onward = [
        remote(tok[2].at[rows_of(c)], tok[3].at[rows_of(c)], f_send.at[c], f_recv.at[c], mates[1])
        for c in range(CHUNKS)
    ]
    for copy in across:
        copy.start()
    beside.start()

    def norm(k, start, count):
        def body(i, carry):
            at_rows = pl.ds(pl.multiple_of(start + i * 16, 16), 16)
            wide = tok[k][at_rows, :].astype(jnp.float32)
            scale = lax.rsqrt(jnp.sum(wide * wide, axis=-1, keepdims=True) * (1.0 / WIDTH) + 1e-05)
            normed[k][at_rows, :] = (wide * scale * gain_ref[...]).astype(jnp.bfloat16)
            return carry

        lax.fori_loop(0, count // 16, body, 0)

    def rotate(value):
        return value * cos_ref[...] + pltpu.roll(value, HW // 2, 1) * sin_ref[...]

    def key_value(k):
        both = jnp.dot(normed[k][...], w[:, 0 : 2 * HW], preferred_element_type=jnp.float32)
        kv[k][z, :, 0:HW] = rotate(both[:, 0:HW]).astype(jnp.bfloat16)
        kv[k][z, :, HW:] = both[:, HW:].astype(jnp.bfloat16)

    def queries(k):
        wide = jnp.dot(normed[k][...], w[:, 2 * HW :], preferred_element_type=jnp.float32)
        for h in range(HEADS):
            qb[k][h * ROWS : (h + 1) * ROWS, :] = rotate(wide[:, h * HW : (h + 1) * HW]).astype(jnp.bfloat16)

    def ring(buf, k, send, recv, up, j):
        place = lax.rem(z - (j - 1) + RING, RING) if up else lax.rem(z + (j - 1), RING)
        index = (k * 2 + (0 if up else 1)) * 4 + j - 1
        return remote(buf.at[place], buf.at[place], send.at[index], recv.at[index], z_up if up else z_down)

    def ring_hops(k):
        return [(up, j) for j in range(1, 5) for up in (True, False) if j < 4 or up == (k % 2 == 0)]

    def ring_step(buf, k, send, recv, j):
        for up, hop in ring_hops(k):
            if hop == j - 1:
                ring(buf, k, send, recv, up, hop).wait_recv()
            if hop == j:
                ring(buf, k, send, recv, up, hop).start()

    def z_step(k, j):
        ring_step(kv[k], k, z_send, z_recv, j)

    def vz_step(k, j):
        ring_step(vz[k], k, vz_send, vz_recv, j)

    def prev_copy(k):
        return remote(kv[k].at[z], prev[k], p_send.at[k], p_recv.at[k], after)

    gives_prev = jnp.logical_and(z == RING - 1, s < LINE - 1)
    takes_prev = jnp.logical_and(z == 0, s > 0)

    def prev_start(k):
        @pl.when(gives_prev)
        def _():
            prev_copy(k).start()

    def prev_wait(k):
        @pl.when(takes_prev)
        def _():
            prev_copy(k).wait_recv()

    def offset(k, t):
        return slash_ref[docs[k] * 16 + g * 4 + t]

    def vertical(k, i):
        return vert_ref[docs[k] * 16 + g * 4 + i]

    def shift(k, t):
        return (offset(k, t) - z + RING - 1) // RING

    def turns(k, t):
        steps = lax.rem(shift(k, t), COLS)
        return steps if t < 2 else lax.rem(COLS - steps, COLS)

    def y_copies(k):
        return [
            remote(ya[k].at[0, 0:2], ya[k].at[1, 0:2], y_send.at[k * 3], y_recv.at[k * 3], y_up),
            remote(ya[k].at[0, 2:4], ya[k].at[1, 2:4], y_send.at[k * 3 + 1], y_recv.at[k * 3 + 1], y_down),
        ]

    def y_second(k):
        return remote(yb[k].at[0], yb[k].at[1], y_send.at[k * 3 + 2], y_recv.at[k * 3 + 2], y_far)

    def y_one(k):
        for t in range(SLOTS):
            ya[k][0, t] = kv[k][lax.rem(z - offset(k, t) + LINE, RING)]
        for copy in y_copies(k):
            copy.start()

    def y_two(k):
        for copy in y_copies(k):
            copy.wait_recv()
        for t in range(SLOTS):
            yb[k][0, t] = ya[k][lax.rem(turns(k, t), 2), t]
        y_second(k).start()

    def x_copy(k):
        return remote(xc[k].at[0], xc[k].at[1], x_send.at[k], x_recv.at[k], x_far)

    def x_one(k):
        y_second(k).wait_recv()
        for t in range(SLOTS):
            xc[k][0, t] = yb[k][turns(k, t) // 2, t]

        @pl.when(x == 0)
        def _():
            x_copy(k).start()

    def x_two(k):
        @pl.when(x == 1)
        def _():
            x_copy(k).wait_recv()

    def vy_copies(k):
        return [
            remote(vy[k].at[y], vy[k].at[y], vy_send.at[k * 3 + i], vy_recv.at[k * 3 + i], device)
            for i, device in enumerate((y_up, y_far, y_down))
        ]

    my_vertical = [vertical(k, lax.rem(z, 4)) for k in range(4)]

    def v_one(k):
        start = pl.multiple_of((z // 4) * 64, 64)
        vy[k][y] = kv[k][lax.rem(my_vertical[k], RING), pl.ds(start, 64), :]
        for copy in vy_copies(k):
            copy.start()

    def vx_copy(k):
        return remote(vx[k].at[0], vx[k].at[1], vx_send.at[k], vx_recv.at[k], x_far)

    def v_two(k):
        for copy in vy_copies(k):
            copy.wait_recv()
        vx[k][0] = vy[k][lax.rem(my_vertical[k] // RING, COLS)]

        @pl.when(x == 0)
        def _():
            vx_copy(k).start()

    def v_three(k):
        @pl.when(x == 1)
        def _():
            vx_copy(k).wait_recv()

        vz[k][z] = vx[k][x * (my_vertical[k] < LINE // 2).astype(jnp.int32)]
        vz_step(k, 1)

    def out_copy(k):
        columns = pl.ds(pl.multiple_of(g * 512, 512), 512)
        if k == 0:
            return pltpu.make_async_copy(ob[0], out_hbm.at[:, columns], local_sem.at[4])
        return remote(ob[k], out_hbm.at[:, columns], o_send.at[k], o_recv.at[k], mates[k])

    low = jnp.float32(-jnp.inf)

    def attend(k):
        def put(i, value):
            kall[i * ROWS : (i + 1) * ROWS, :] = value[:, 0:HW]
            vall[i * ROWS : (i + 1) * ROWS, :] = value[:, HW:]

        put(0, kv[k][z])

        @pl.when(z > 0)
        def _():
            put(1, kv[k][lax.rem(z + RING - 1, RING)])

        @pl.when(takes_prev)
        def _():
            put(1, prev[k][...])

        @pl.when(s == 0)
        def _():
            put(1, jnp.zeros((ROWS, 2 * HW), jnp.bfloat16))

        bias = [jnp.float32(0.0), jnp.where(s >= 1, jnp.float32(0.0), low)]
        for t in range(SLOTS):
            other = x * (shift(k, t) > y).astype(jnp.int32)
            put(2 + t, xc[k][other, t])
            bias.append(jnp.where(s >= offset(k, t), jnp.float32(0.0), low))
        for i in range(4):
            at_block = (2 + SLOTS + i) * ROWS
            for half in range(2):
                value = vz[k][i + 4 * half]
                kall[at_block + half * 64 : at_block + half * 64 + 64, :] = value[:, 0:HW]
                vall[at_block + half * 64 : at_block + half * 64 + 64, :] = value[:, HW:]
            block = vertical(k, i)
            good = block < s - 1
            for t in range(SLOTS):
                good = jnp.logical_and(good, block != s - offset(k, t))
            bias.append(jnp.where(good, jnp.float32(0.0), low))
        blocks = len(bias)
        causal = lax.broadcasted_iota(jnp.int32, (ROWS, ROWS), 1) <= lax.broadcasted_iota(jnp.int32, (ROWS, ROWS), 0)

        def head(h, carry):
            query = qb[k][pl.ds(pl.multiple_of(h * ROWS, ROWS), ROWS), :]
            scores = lax.dot_general(
                query, kall[...], (((1,), (1,)), ((), ())), preferred_element_type=jnp.float32
            ) * (HW ** (-0.5))
            tiles = [scores[:, i * ROWS : (i + 1) * ROWS] for i in range(blocks)]
            tiles = [jnp.where(causal, tiles[0], low)] + [tiles[i] + bias[i] for i in range(1, blocks)]
            highest = tiles[0]
            for tile in tiles[1:]:
                highest = jnp.maximum(highest, tile)
            highest = jnp.max(highest, axis=1, keepdims=True)
            raised = [jnp.exp(tile - highest) for tile in tiles]
            total = raised[0]
            for tile in raised[1:]:
                total = total + tile
            total = jnp.sum(total, axis=1, keepdims=True)
            weights = jnp.concatenate([tile.astype(jnp.bfloat16) for tile in raised], axis=1)
            mixed = jnp.dot(weights, vall[...], preferred_element_type=jnp.float32) / total
            ob[k][:, pl.ds(pl.multiple_of(h * HW, HW), HW)] = mixed.astype(jnp.bfloat16)
            return carry

        lax.fori_loop(0, HEADS, head, 0)
        out_copy(k).start()

    def arrive(c):
        across[c].wait_recv()
        onward[c].start()
        norm(2, c * part, part)

    loads[0].wait()
    norm(0, 0, ROWS)
    loads[1].wait()
    loads[2].wait()
    key_value(0)
    z_step(0, 1)
    prev_start(0)
    beside.wait_recv()
    norm(1, 0, ROWS)
    key_value(1)
    z_step(1, 1)
    prev_start(1)
    loads[3].wait()
    queries(0)
    z_step(0, 2)
    z_step(1, 2)
    arrive(0)
    queries(1)
    z_step(0, 3)
    z_step(1, 3)
    z_step(0, 4)
    z_step(1, 4)
    arrive(1)
    z_step(0, 5)
    y_one(0)
    v_one(0)
    z_step(1, 5)
    y_one(1)
    v_one(1)
    arrive(2)
    y_two(0)
    y_two(1)
    v_two(0)
    v_two(1)
    arrive(3)
    key_value(2)
    z_step(2, 1)
    prev_start(2)
    for copy in onward:
        copy.wait_recv()
    norm(3, 0, ROWS)
    key_value(3)
    z_step(3, 1)
    prev_start(3)
    x_one(0)
    v_three(0)
    z_step(2, 2)
    x_one(1)
    v_three(1)
    z_step(3, 2)
    queries(2)
    z_step(2, 3)
    z_step(3, 3)
    vz_step(0, 2)
    vz_step(1, 2)
    queries(3)
    z_step(2, 4)
    z_step(3, 4)
    vz_step(0, 3)
    vz_step(1, 3)
    z_step(2, 5)
    y_one(2)
    v_one(2)
    z_step(3, 5)
    y_one(3)
    v_one(3)
    for j in (4, 5):
        vz_step(0, j)
        vz_step(1, j)
    prev_wait(0)
    x_two(0)
    attend(0)
    y_two(2)
    v_two(2)
    y_two(3)
    v_two(3)
    prev_wait(1)
    x_two(1)
    attend(1)
    x_one(2)
    v_three(2)
    x_one(3)
    v_three(3)
    for j in (2, 3, 4, 5):
        vz_step(2, j)
        vz_step(3, j)
    prev_wait(2)
    x_two(2)
    attend(2)
    prev_wait(3)
    x_two(3)
    attend(3)

    for copy in across + [beside] + onward:
        copy.wait_send()
    for k in range(4):
        for up, j in ring_hops(k):
            ring(kv[k], k, z_send, z_recv, up, j).wait_send()
            ring(vz[k], k, vz_send, vz_recv, up, j).wait_send()
        for copy in y_copies(k) + [y_second(k)] + vy_copies(k):
            copy.wait_send()

        @pl.when(gives_prev)
        def _():
            prev_copy(k).wait_send()

        @pl.when(x == 0)
        def _():
            x_copy(k).wait_send()
            vx_copy(k).wait_send()

    for k in range(4):
        out_copy(k).wait()


def local(tokens, norm_gain, w_query, key_weight, value_weight, vertical_blocks, slash_offsets):
    cosine, sine = rope_tables(lax.axis_index("seq"))
    bf16 = jnp.bfloat16
    unit = (ROWS, 2 * HW)
    dma = pltpu.SemaphoreType.DMA

    def many(shape):
        return [pltpu.VMEM(shape, bf16)] * DOCS

    scratch = (
        many((ROWS, WIDTH))
        + many((ROWS, WIDTH))
        + [pltpu.VMEM((WIDTH, 6 * HW), bf16)]
        + many((RING,) + unit)
        + many(unit)
        + many((2, SLOTS) + unit)
        + many((2, SLOTS) + unit)
        + many((2, SLOTS) + unit)
        + many((COLS, 64, 2 * HW))
        + many((2, 64, 2 * HW))
        + many((RING, 64, 2 * HW))
        + many((HEADS * ROWS, HW))
        + [pltpu.VMEM((10 * ROWS, HW), bf16)] * 2
        + many((ROWS, HEADS * HW))
        + [dma((5,))]
        + [dma((CHUNKS + 1,))] * 2
        + [dma((CHUNKS,))] * 2
        + [dma((4,))] * 2
        + [dma((32,))] * 2
        + [dma((12,))] * 2
        + [dma((4,))] * 2
        + [dma((12,))] * 2
        + [dma((4,))] * 2
        + [dma((32,))] * 2
        + [dma((4,))] * 2
    )
    smem = pl.BlockSpec(memory_space=pltpu.SMEM)
    vmem = pl.BlockSpec(memory_space=pltpu.VMEM)
    hbm = pl.BlockSpec(memory_space=pl.ANY)
    out = pl.pallas_call(
        kernel,
        out_shape=jax.ShapeDtypeStruct((ROWS, DOCS * HEADS * HW), bf16),
        in_specs=[smem, smem, hbm, vmem, hbm, hbm, hbm, vmem, vmem],
        out_specs=hbm,
        scratch_shapes=scratch,
        compiler_params=pltpu.CompilerParams(
            collective_id=0, has_side_effects=True, vmem_limit_bytes=60 * 1024 * 1024
        ),
    )(
        vertical_blocks.reshape(-1),
        slash_offsets.reshape(-1),
        tokens[0],
        norm_gain[None, :],
        w_query,
        key_weight,
        value_weight,
        cosine,
        sine,
    )
    return out[None]


def solution(mesh):
    return jax.shard_map(
        local,
        mesh=mesh,
        in_specs=(
            P("doc", "seq", None),
            P(),
            P(None, "doc"),
            P(None, "doc"),
            P(None, "doc"),
            P(),
            P(),
        ),
        out_specs=P("doc", "seq", None),
        check_vma=False,
    )
```

```python
import functools

import jax
import jax.numpy as jnp
from jax import lax
from jax.experimental import pallas as pl
from jax.experimental.pallas import tpu as pltpu
from jax.sharding import PartitionSpec as P

MESH = pl.DeviceIdType.MESH
HEADS = 4
HW = 128
ROWS = 128
WIDTH = 4096
DOCS = 4
RING = 8
COLS = 4
SLOTS = 4
CHUNKS = 4
PART = ROWS // CHUNKS
LINE = 64

PLAN = [
    ("own", 0), ("kv", 0), ("z", 0, 1), ("prev", 0),
    ("beside", 1), ("kv", 1), ("z", 1, 1), ("prev", 1),
    ("arrive", 2, 0), ("z", 0, 2), ("z", 1, 2), ("q", 0),
    ("arrive", 2, 1), ("z", 0, 3), ("z", 1, 3),
    ("arrive", 2, 2), ("z", 0, 4), ("z", 1, 4), ("q", 1),
    ("arrive", 2, 3), ("kv", 2), ("z", 2, 1), ("prev", 2),
    ("z", 0, 5), ("y1", 0), ("v1", 0), ("z", 1, 5), ("y1", 1), ("v1", 1), ("z", 2, 2),
    ("arrive", 3, 0), ("z", 2, 3), ("y2", 0), ("v2", 0),
    ("arrive", 3, 1), ("z", 2, 4), ("y2", 1), ("v2", 1), ("q", 2), ("z", 2, 5), ("y1", 2), ("v1", 2),
    ("arrive", 3, 2),
    ("arrive", 3, 3), ("kv", 3), ("z", 3, 1), ("prev", 3),
    ("x1", 0), ("v3", 0), ("x1", 1), ("v3", 1), ("z", 3, 2), ("y2", 2), ("v2", 2),
    ("vz", 0, 2), ("vz", 1, 2), ("z", 3, 3), ("vz", 0, 3), ("vz", 1, 3), ("q", 3),
    ("z", 3, 4), ("x1", 2), ("v3", 2), ("z", 3, 5), ("y1", 3), ("v1", 3),
    ("vz", 0, 4), ("vz", 1, 4), ("vz", 0, 5), ("vz", 1, 5), ("attend", 0),
    ("y2", 3), ("v2", 3), ("vz", 2, 2), ("attend", 1), ("vz", 2, 3), ("x1", 3), ("v3", 3),
    ("vz", 2, 4), ("vz", 2, 5), ("vz", 3, 2), ("attend", 2),
    ("vz", 3, 3), ("vz", 3, 4), ("vz", 3, 5), ("attend", 3),
]


def rope_tables(place):
    positions = place * ROWS + jnp.arange(ROWS, dtype=jnp.int32)
    inverse = jnp.power(jnp.float32(500000.0), -jnp.arange(0, HW, 2, dtype=jnp.float32) / HW)
    angles = positions.astype(jnp.float32)[:, None] * inverse[None, :]
    cosine, sine = jnp.cos(angles), jnp.sin(angles)
    return jnp.concatenate([cosine, cosine], axis=1), jnp.concatenate([-sine, sine], axis=1)


def take(refs, *counts):
    refs = list(refs)
    out = []
    for count in counts:
        out.append(refs[:count] if count > 1 else refs[0])
        del refs[:count]
    return out


def guarded(condition, act):
    if condition is None:
        act()
    else:
        pl.when(condition)(act)


class Copy:
    def __init__(self, log, src, dst, send, recv, device, sends=None, takes=None):
        self.log, self.parts = log, (src, dst, send, recv, device)
        self.sends, self.takes = sends, takes
        self.landed = False

    def make(self):
        src, dst, send, recv, device = self.parts
        return pltpu.make_async_remote_copy(
            src_ref=src, dst_ref=dst, send_sem=send, recv_sem=recv, device_id=device, device_id_type=MESH
        )

    def start(self):
        guarded(self.sends, lambda: self.make().start())
        self.log.append(self)

    def land(self):
        guarded(self.takes, lambda: self.make().wait_recv())
        self.landed = True

    def sent(self):
        guarded(self.sends, lambda: self.make().wait_send())


def kernel(plan, vert_ref, slash_ref, tok_hbm, gain_ref, wq_hbm, wk_hbm, wv_hbm, cos_ref, sin_ref, out_hbm, *scratch):
    (
        tok, normed, w, kv, prev, ya, yb, xc, vy, vx, vz, qb, kall, vall, ob,
        local_sem, t_send, t_recv, f_send, p_send, p_recv, z_send, z_recv, y_send, y_recv,
        x_send, x_recv, vy_send, vy_recv, vx_send, vx_recv, vz_send, vz_recv, o_send, o_recv,
    ) = take(scratch, 4, 4, 1, 4, 4, 4, 4, 4, 4, 4, 4, 4, 1, 1, 4, *([1] * 20))
    s = lax.axis_index("seq")
    g = lax.axis_index("doc")
    core = lax.rem(g, 2)
    z = lax.rem(s, RING)
    row = s // RING
    y = lax.rem(row, COLS)
    x = row // COLS
    across = lax.rem(g - core + 2, 4)
    docs = [g, g + 1 - 2 * core, across, across + 1]

    def at(seq, doc):
        return {"seq": seq, "doc": doc}

    z_up = at(s - z + lax.rem(z + 1, RING), g)
    z_down = at(s - z + lax.rem(z + RING - 1, RING), g)
    y_up = at(s - y * RING + lax.rem(y + 1, COLS) * RING, g)
    y_far = at(s - y * RING + lax.rem(y + 2, COLS) * RING, g)
    y_down = at(s - y * RING + lax.rem(y + 3, COLS) * RING, g)
    x_far = at(lax.rem(s + LINE // 2, LINE), g)
    after = at(lax.rem(s + 1, LINE), g)
    before = at(lax.rem(s + LINE - 1, LINE), g)
    mates = [at(s, doc) for doc in docs]
    peer = at(s, across + core)

    log = []

    def remote(*parts, **ends):
        return Copy(log, *parts, **ends)

    loads = [
        pltpu.make_async_copy(tok_hbm, tok[0], local_sem.at[0]),
        pltpu.make_async_copy(wk_hbm, w.at[:, 0:HW], local_sem.at[1]),
        pltpu.make_async_copy(wv_hbm, w.at[:, HW : 2 * HW], local_sem.at[2]),
        pltpu.make_async_copy(wq_hbm, w.at[:, 2 * HW :], local_sem.at[3]),
    ]
    for load in loads:
        load.start()

    barrier = pltpu.get_barrier_semaphore()
    greeted = mates[1:] + [z_up, z_down, y_up, y_far, y_down, x_far, after, before]
    for device in greeted:
        pl.semaphore_signal(barrier, inc=1, device_id=device, device_id_type=MESH)
    pl.semaphore_wait(barrier, len(greeted))

    even, odd = core == 0, core == 1
    lower, upper = x == 0, x == 1
    gives_prev = jnp.logical_and(z == RING - 1, s < LINE - 1)
    takes_prev = jnp.logical_and(z == 0, s > 0)

    def rows_of(c):
        return pl.ds(c * PART, PART)

    def chunk_sem(k, c):
        return t_recv.at[(k - 2) * CHUNKS + c]

    crossing = [
        [
            remote(
                tok_hbm.at[rows_of(c)], tok[k].at[rows_of(c)], t_send.at[c], chunk_sem(k, c), peer,
                sends=even if k == 2 else odd,
            )
            for c in range(CHUNKS)
        ]
        for k in (2, 3)
    ]
    handed = [
        [
            remote(
                tok[k].at[rows_of(c)], tok[k].at[rows_of(c)], f_send.at[c], chunk_sem(k, c), mates[1],
                sends=even if k == 2 else odd,
            )
            for c in range(CHUNKS)
        ]
        for k in (2, 3)
    ]
    beside = remote(tok_hbm, tok[1], t_send.at[CHUNKS], t_recv.at[2 * CHUNKS], mates[1])

    def norm(k, start, count):
        def body(i, carry):
            at_rows = pl.ds(pl.multiple_of(start + i * 16, 16), 16)
            wide = tok[k][at_rows, :].astype(jnp.float32)
            scale = lax.rsqrt(jnp.sum(wide * wide, axis=-1, keepdims=True) * (1.0 / WIDTH) + 1e-05)
            normed[k][at_rows, :] = (wide * scale * gain_ref[...]).astype(jnp.bfloat16)
            return carry

        lax.fori_loop(0, count // 16, body, 0)

    def do_own(k):
        loads[0].wait()
        norm(0, 0, ROWS)

    def do_beside(k):
        beside.land()
        norm(1, 0, ROWS)

    def do_arrive(k, c):
        crossing[k - 2][c].land()
        handed[k - 2][c].start()
        handed[k - 2][c].landed = True
        if k == 2 and c == CHUNKS - 2:
            for copy in crossing[1]:
                copy.start()
        norm(k, c * PART, PART)

    def rotate(value):
        return value * cos_ref[...] + pltpu.roll(value, HW // 2, 1) * sin_ref[...]

    ready = set()

    def loaded(*which):
        for i in which:
            if i not in ready:
                loads[i].wait()
                ready.add(i)

    def do_kv(k):
        loaded(1, 2)
        both = jnp.dot(normed[k][...], w[:, 0 : 2 * HW], preferred_element_type=jnp.float32)
        kv[k][z, :, 0:HW] = rotate(both[:, 0:HW]).astype(jnp.bfloat16)
        kv[k][z, :, HW:] = both[:, HW:].astype(jnp.bfloat16)

    def do_q(k):
        loaded(3)
        wide = jnp.dot(normed[k][...], w[:, 2 * HW :], preferred_element_type=jnp.float32)
        for h in range(HEADS):
            qb[k][h * ROWS : (h + 1) * ROWS, :] = rotate(wide[:, h * HW : (h + 1) * HW]).astype(jnp.bfloat16)

    def ring(buf, k, send, recv):
        hops = {}
        for j in range(1, 5):
            for up in (True, False):
                if j == 4 and up != (k % 2 == 0):
                    continue
                place = lax.rem(z - (j - 1) + RING, RING) if up else lax.rem(z + (j - 1), RING)
                index = (k * 2 + (0 if up else 1)) * 4 + j - 1
                hops[up, j] = remote(
                    buf.at[place], buf.at[place], send.at[index], recv.at[index], z_up if up else z_down
                )
        return hops

    z_hops = [ring(kv[k], k, z_send, z_recv) for k in range(DOCS)]
    vz_hops = [ring(vz[k], k, vz_send, vz_recv) for k in range(DOCS)]

    def step(hops, j):
        for up in (True, False):
            if (up, j - 1) in hops:
                hops[up, j - 1].land()
            if (up, j) in hops:
                hops[up, j].start()

    def do_z(k, j):
        step(z_hops[k], j)

    def do_vz(k, j):
        step(vz_hops[k], j)

    prevs = [
        remote(kv[k].at[z], prev[k], p_send.at[k], p_recv.at[k], after, sends=gives_prev, takes=takes_prev)
        for k in range(DOCS)
    ]

    def do_prev(k):
        prevs[k].start()

    offset = [[slash_ref[docs[k], g, t] for t in range(SLOTS)] for k in range(DOCS)]
    vertical = [[vert_ref[docs[k], g, i] for i in range(4)] for k in range(DOCS)]
    mine = [vert_ref[docs[k], g, lax.rem(z, 4)] for k in range(DOCS)]
    shift = [[(offset[k][t] - z + RING - 1) // RING for t in range(SLOTS)] for k in range(DOCS)]

    def turns(k, t):
        steps = lax.rem(shift[k][t], COLS)
        return steps if t < 2 else lax.rem(COLS - steps, COLS)

    y_near = [
        [
            remote(ya[k].at[0, 0:2], ya[k].at[1, 0:2], y_send.at[k * 3], y_recv.at[k * 3], y_up),
            remote(ya[k].at[0, 2:4], ya[k].at[1, 2:4], y_send.at[k * 3 + 1], y_recv.at[k * 3 + 1], y_down),
        ]
        for k in range(DOCS)
    ]
    y_over = [
        remote(yb[k].at[0], yb[k].at[1], y_send.at[k * 3 + 2], y_recv.at[k * 3 + 2], y_far) for k in range(DOCS)
    ]
    x_over = [
        remote(xc[k].at[0], xc[k].at[1], x_send.at[k], x_recv.at[k], x_far, sends=lower, takes=upper)
        for k in range(DOCS)
    ]
    vy_over = [
        [
            remote(vy[k].at[y], vy[k].at[y], vy_send.at[k * 3 + i], vy_recv.at[k * 3 + i], device)
            for i, device in enumerate((y_up, y_far, y_down))
        ]
        for k in range(DOCS)
    ]
    vx_over = [
        remote(vx[k].at[0], vx[k].at[1], vx_send.at[k], vx_recv.at[k], x_far, sends=lower, takes=upper)
        for k in range(DOCS)
    ]

    def do_y1(k):
        for t in range(SLOTS):
            ya[k][0, t] = kv[k][lax.rem(z - offset[k][t] + LINE, RING)]
        for copy in y_near[k]:
            copy.start()

    def do_y2(k):
        for copy in y_near[k]:
            copy.land()
        for t in range(SLOTS):
            yb[k][0, t] = ya[k][lax.rem(turns(k, t), 2), t]
        y_over[k].start()

    def do_x1(k):
        y_over[k].land()
        for t in range(SLOTS):
            xc[k][0, t] = yb[k][turns(k, t) // 2, t]
        x_over[k].start()

    def do_v1(k):
        start = pl.multiple_of((z // 4) * 64, 64)
        vy[k][y] = kv[k][lax.rem(mine[k], RING), pl.ds(start, 64), :]
        for copy in vy_over[k]:
            copy.start()

    def do_v2(k):
        for copy in vy_over[k]:
            copy.land()
        vx[k][0] = vy[k][lax.rem(mine[k] // RING, COLS)]
        vx_over[k].start()

    def do_v3(k):
        vx_over[k].land()
        vz[k][z] = vx[k][x * (mine[k] < LINE // 2).astype(jnp.int32)]
        do_vz(k, 1)

    columns = pl.ds(pl.multiple_of(g * 512, 512), 512)
    out_own = pltpu.make_async_copy(ob[0], out_hbm.at[:, columns], local_sem.at[4])
    out_sent = [None] + [
        remote(ob[k], out_hbm.at[:, columns], o_send.at[k], o_recv.at[0 if k == 1 else 1 + core], mates[k])
        for k in range(1, DOCS)
    ]
    out_got = [remote(ob[1], out_hbm.at[:, columns], o_send.at[1], o_recv.at[i], mates[1]) for i in range(3)]

    low = jnp.float32(-jnp.inf)

    def do_attend(k):
        prevs[k].land()
        x_over[k].land()

        def put(i, value):
            kall[i * ROWS : (i + 1) * ROWS, :] = value[:, 0:HW]
            vall[i * ROWS : (i + 1) * ROWS, :] = value[:, HW:]

        put(0, kv[k][z])

        @pl.when(z > 0)
        def _():
            put(1, kv[k][lax.rem(z + RING - 1, RING)])

        @pl.when(takes_prev)
        def _():
            put(1, prev[k][...])

        @pl.when(s == 0)
        def _():
            put(1, jnp.zeros((ROWS, 2 * HW), jnp.bfloat16))

        bias = [jnp.float32(0.0), jnp.where(s >= 1, jnp.float32(0.0), low)]
        for t in range(SLOTS):
            other = x * (shift[k][t] > y).astype(jnp.int32)
            put(2 + t, xc[k][other, t])
            bias.append(jnp.where(s >= offset[k][t], jnp.float32(0.0), low))
        for i in range(4):
            at_block = (2 + SLOTS + i) * ROWS
            for half in range(2):
                value = vz[k][i + 4 * half]
                kall[at_block + half * 64 : at_block + half * 64 + 64, :] = value[:, 0:HW]
                vall[at_block + half * 64 : at_block + half * 64 + 64, :] = value[:, HW:]
            block = vertical[k][i]
            good = block < s - 1
            for t in range(SLOTS):
                good = jnp.logical_and(good, block != s - offset[k][t])
            bias.append(jnp.where(good, jnp.float32(0.0), low))
        blocks = len(bias)
        causal = lax.broadcasted_iota(jnp.int32, (ROWS, ROWS), 1) <= lax.broadcasted_iota(jnp.int32, (ROWS, ROWS), 0)

        def head(h, carry):
            query = qb[k][pl.ds(pl.multiple_of(h * ROWS, ROWS), ROWS), :]
            scores = lax.dot_general(
                query, kall[...], (((1,), (1,)), ((), ())), preferred_element_type=jnp.float32
            ) * (HW ** (-0.5))
            tiles = [scores[:, i * ROWS : (i + 1) * ROWS] for i in range(blocks)]
            tiles = [jnp.where(causal, tiles[0], low)] + [tiles[i] + bias[i] for i in range(1, blocks)]
            highest = tiles[0]
            for tile in tiles[1:]:
                highest = jnp.maximum(highest, tile)
            highest = jnp.max(highest, axis=1, keepdims=True)
            raised = [jnp.exp(tile - highest) for tile in tiles]
            total = raised[0]
            for tile in raised[1:]:
                total = total + tile
            total = jnp.sum(total, axis=1, keepdims=True)
            weights = jnp.concatenate([tile.astype(jnp.bfloat16) for tile in raised], axis=1)
            mixed = jnp.dot(weights, vall[...], preferred_element_type=jnp.float32) / total
            ob[k][:, pl.ds(pl.multiple_of(h * HW, HW), HW)] = mixed.astype(jnp.bfloat16)
            return carry

        lax.fori_loop(0, HEADS, head, 0)
        if k == 0:
            out_own.start()
        else:
            out_sent[k].start()
            out_sent[k].landed = True

    for copy in crossing[0]:
        copy.start()
    beside.start()
    does = {
        "own": do_own, "beside": do_beside, "arrive": do_arrive, "kv": do_kv, "q": do_q, "z": do_z, "vz": do_vz,
        "prev": do_prev, "y1": do_y1, "y2": do_y2, "x1": do_x1, "v1": do_v1, "v2": do_v2, "v3": do_v3,
        "attend": do_attend,
    }
    for name, *which in plan:
        does[name](*which)

    loaded(1, 2, 3)
    for copy in log:
        if not copy.landed:
            copy.land()
        copy.sent()
    if ("attend", 0) in plan:
        out_own.wait()
    for i in range(3):
        if ("attend", i + 1) in plan:
            out_got[i].land()


def layer(plan, collective_id, tokens, norm_gain, w_query, key_weight, value_weight, vertical_blocks, slash_offsets):
    cosine, sine = rope_tables(lax.axis_index("seq"))
    bf16 = jnp.bfloat16
    unit = (ROWS, 2 * HW)
    dma = pltpu.SemaphoreType.DMA

    def many(shape):
        return [pltpu.VMEM(shape, bf16)] * DOCS

    scratch = (
        many((ROWS, WIDTH))
        + many((ROWS, WIDTH))
        + [pltpu.VMEM((WIDTH, 6 * HW), bf16)]
        + many((RING,) + unit)
        + many(unit)
        + many((2, SLOTS) + unit) * 3
        + many((COLS, 64, 2 * HW))
        + many((2, 64, 2 * HW))
        + many((RING, 64, 2 * HW))
        + many((HEADS * ROWS, HW))
        + [pltpu.VMEM((10 * ROWS, HW), bf16)] * 2
        + many((ROWS, HEADS * HW))
        + [dma((5,)), dma((CHUNKS + 1,)), dma((2 * CHUNKS + 1,)), dma((CHUNKS,))]
    )
    for count in (4, 32, 12, 4, 12, 4, 32, 4):
        scratch += [dma((count,))] * 2
    smem = pl.BlockSpec(memory_space=pltpu.SMEM)
    vmem = pl.BlockSpec(memory_space=pltpu.VMEM)
    hbm = pl.BlockSpec(memory_space=pl.ANY)
    out = pl.pallas_call(
        functools.partial(kernel, plan),
        out_shape=jax.ShapeDtypeStruct((ROWS, DOCS * HEADS * HW), bf16),
        in_specs=[smem, smem, hbm, vmem, hbm, hbm, hbm, vmem, vmem],
        out_specs=hbm,
        scratch_shapes=scratch,
        compiler_params=pltpu.CompilerParams(
            collective_id=collective_id, has_side_effects=True, vmem_limit_bytes=60 * 1024 * 1024
        ),
    )(
        vertical_blocks, slash_offsets, tokens[0], norm_gain[None, :], w_query, key_weight, value_weight, cosine, sine
    )
    return out[None]


IN_SPECS = (
    P("doc", "seq", None),
    P(),
    P(None, "doc"),
    P(None, "doc"),
    P(None, "doc"),
    P(),
    P(),
)


def solution(mesh):
    return jax.shard_map(
        functools.partial(layer, PLAN, 0),
        mesh=mesh,
        in_specs=IN_SPECS,
        out_specs=P("doc", "seq", None),
        check_vma=False,
    )
```

```python
import functools

import jax
import jax.numpy as jnp
from jax import lax
from jax.experimental import pallas as pl
from jax.experimental.pallas import tpu as pltpu
from jax.sharding import PartitionSpec as P

MESH = pl.DeviceIdType.MESH
HEADS = 4
HW = 128
ROWS = 128
HALF = ROWS // 2
WIDTH = 4096
DOCS = 4
UNITS = 2 * DOCS
RING = 8
COLS = 4
SLOTS = 4
CHUNKS = 4
PART = ROWS // CHUNKS
LINE = 64

PLAN = [
    ("own", 0), ("kv", 0, 0), ("kv", 0, 1), ("z", 0, 0, 1), ("prev", 0, 0), ("z", 0, 1, 1), ("prev", 0, 1), ("q", 0),
    ("beside", 1), ("kv", 1, 0), ("arrive", 2, 0), ("kv", 1, 1), ("z", 1, 0, 1), ("prev", 1, 0), ("z", 1, 1, 1),
    ("prev", 1, 1), ("z", 0, 0, 2), ("z", 0, 1, 2), ("q", 1), ("arrive", 2, 1), ("kv", 2, 0), ("z", 2, 0, 1),
    ("prev", 2, 0), ("z", 1, 0, 2), ("z", 1, 1, 2), ("z", 0, 0, 3), ("z", 0, 1, 3), ("arrive", 2, 2), ("z", 2, 0, 2),
    ("z", 1, 0, 3), ("z", 1, 1, 3), ("z", 0, 0, 4), ("arrive", 2, 3), ("kv", 2, 1), ("z", 2, 1, 1), ("prev", 2, 1),
    ("z", 0, 1, 4), ("q", 2), ("z", 2, 0, 3), ("z", 1, 0, 4), ("z", 1, 1, 4), ("z", 0, 0, 5), ("y1", 0, 0),
    ("arrive", 3, 0), ("z", 0, 1, 5), ("z", 2, 1, 2), ("v1", 0), ("y1", 0, 1), ("z", 2, 0, 4), ("z", 1, 0, 5),
    ("z", 1, 1, 5), ("v1", 1), ("y1", 1, 0), ("y1", 1, 1), ("arrive", 3, 1), ("kv", 3, 0), ("z", 3, 0, 1),
    ("prev", 3, 0), ("z", 2, 1, 3), ("y2", 0, 0), ("z", 2, 0, 5), ("y1", 2, 0), ("arrive", 3, 2), ("y2", 0, 1),
    ("z", 3, 0, 2), ("z", 2, 1, 4), ("arrive", 3, 3), ("kv", 3, 1), ("z", 3, 0, 3), ("z", 3, 1, 1), ("prev", 3, 1),
    ("z", 2, 1, 5), ("v1", 2), ("y1", 2, 1), ("v2", 1), ("y2", 1, 0), ("v2", 0), ("q", 3), ("y2", 1, 1),
    ("z", 3, 0, 4), ("z", 3, 1, 2), ("v3", 1), ("v3", 0), ("x1", 0, 0), ("z", 3, 0, 5), ("y1", 3, 0), ("y2", 2, 0),
    ("z", 3, 1, 3), ("vz", 1, 2), ("vz", 0, 2), ("z", 3, 1, 4), ("vz", 1, 3), ("x1", 0, 1), ("vz", 0, 3), ("v2", 2),
    ("z", 3, 1, 5), ("v1", 3), ("y1", 3, 1), ("y2", 2, 1), ("vz", 1, 4), ("vz", 0, 4), ("vz", 1, 5), ("vz", 0, 5),
    ("stage", 0), ("x1", 1, 0), ("v3", 2), ("head", 0, 0), ("head", 0, 1), ("head", 0, 2), ("vz", 2, 2),
    ("x1", 1, 1), ("head", 0, 3), ("y2", 3, 0), ("vz", 2, 3), ("x1", 2, 0), ("vz", 2, 4), ("stage", 1), ("v2", 3),
    ("head", 1, 0), ("y2", 3, 1), ("head", 1, 1), ("vz", 2, 5), ("head", 1, 2), ("head", 1, 3), ("x1", 2, 1),
    ("v3", 3), ("vz", 3, 2), ("x1", 3, 0), ("vz", 3, 3), ("stage", 2), ("x1", 3, 1), ("head", 2, 0), ("head", 2, 1),
    ("vz", 3, 4), ("head", 2, 2), ("head", 2, 3), ("vz", 3, 5), ("stage", 3), ("head", 3, 0), ("head", 3, 1),
    ("head", 3, 2), ("head", 3, 3),
]


def rope_tables(place):
    positions = place * ROWS + jnp.arange(ROWS, dtype=jnp.int32)
    inverse = jnp.power(jnp.float32(500000.0), -jnp.arange(0, HW, 2, dtype=jnp.float32) / HW)
    angles = positions.astype(jnp.float32)[:, None] * inverse[None, :]
    cosine, sine = jnp.cos(angles), jnp.sin(angles)
    return jnp.concatenate([cosine, cosine], axis=1), jnp.concatenate([-sine, sine], axis=1)


def take(refs, *counts):
    refs = list(refs)
    out = []
    for count in counts:
        out.append(refs[:count] if count > 1 else refs[0])
        del refs[:count]
    return out


def guarded(condition, act):
    if condition is None:
        act()
    else:
        pl.when(condition)(act)


class Copy:
    def __init__(self, log, src, dst, send, recv, device, sends=None, takes=None):
        self.log, self.parts = log, (src, dst, send, recv, device)
        self.sends, self.takes = sends, takes
        self.landed = False

    def make(self):
        src, dst, send, recv, device = self.parts
        return pltpu.make_async_remote_copy(
            src_ref=src, dst_ref=dst, send_sem=send, recv_sem=recv, device_id=device, device_id_type=MESH
        )

    def start(self):
        guarded(self.sends, lambda: self.make().start())
        self.log.append(self)

    def land(self):
        guarded(self.takes, lambda: self.make().wait_recv())
        self.landed = True

    def sent(self):
        guarded(self.sends, lambda: self.make().wait_send())


def kernel(plan, vert_ref, slash_ref, tok_hbm, gain_ref, wq_hbm, wk_hbm, wv_hbm, cos_ref, sin_ref, out_hbm, *scratch):
    (
        tok, normed, w, kv, prev, ya, yb, xc, vy, vx, vz, qb, kall, vall, ob,
        local_sem, t_send, t_recv, f_send, p_send, p_recv, z_send, z_recv, y_send, y_recv,
        x_send, x_recv, vy_send, vy_recv, vx_send, vx_recv, vz_send, vz_recv, o_send, o_recv,
    ) = take(scratch, 4, 4, 1, 8, 8, 8, 8, 8, 4, 4, 4, 4, 1, 1, 4, *([1] * 20))
    s = lax.axis_index("seq")
    g = lax.axis_index("doc")
    core = lax.rem(g, 2)
    z = lax.rem(s, RING)
    row = s // RING
    y = lax.rem(row, COLS)
    x = row // COLS
    across = lax.rem(g - core + 2, 4)
    docs = [g, g + 1 - 2 * core, across, across + 1]

    def at(seq, doc):
        return {"seq": seq, "doc": doc}

    z_up = at(s - z + lax.rem(z + 1, RING), g)
    z_down = at(s - z + lax.rem(z + RING - 1, RING), g)
    y_up = at(s - y * RING + lax.rem(y + 1, COLS) * RING, g)
    y_far = at(s - y * RING + lax.rem(y + 2, COLS) * RING, g)
    y_down = at(s - y * RING + lax.rem(y + 3, COLS) * RING, g)
    x_far = at(lax.rem(s + LINE // 2, LINE), g)
    after = at(lax.rem(s + 1, LINE), g)
    before = at(lax.rem(s + LINE - 1, LINE), g)
    mates = [at(s, doc) for doc in docs]
    peer = at(s, across + core)

    log = []

    def remote(*parts, **ends):
        return Copy(log, *parts, **ends)

    loads = [
        pltpu.make_async_copy(tok_hbm, tok[0], local_sem.at[0]),
        pltpu.make_async_copy(wk_hbm, w.at[:, 0:HW], local_sem.at[1]),
        pltpu.make_async_copy(wv_hbm, w.at[:, HW : 2 * HW], local_sem.at[2]),
        pltpu.make_async_copy(wq_hbm, w.at[:, 2 * HW :], local_sem.at[3]),
    ]
    for load in loads:
        load.start()

    barrier = pltpu.get_barrier_semaphore()
    greeted = mates[1:] + [z_up, z_down, y_up, y_far, y_down, x_far, after, before]
    for device in greeted:
        pl.semaphore_signal(barrier, inc=1, device_id=device, device_id_type=MESH)
    pl.semaphore_wait(barrier, len(greeted))

    even, odd = core == 0, core == 1
    lower, upper = x == 0, x == 1
    gives_prev = jnp.logical_and(z == RING - 1, s < LINE - 1)
    takes_prev = jnp.logical_and(z == 0, s > 0)

    def rows_of(c):
        return pl.ds(c * PART, PART)

    def chunk_sem(k, c):
        return t_recv.at[(k - 2) * CHUNKS + c]

    crossing = [
        [
            remote(
                tok_hbm.at[rows_of(c)], tok[k].at[rows_of(c)], t_send.at[c], chunk_sem(k, c), peer,
                sends=even if k == 2 else odd,
            )
            for c in range(CHUNKS)
        ]
        for k in (2, 3)
    ]
    handed = [
        [
            remote(
                tok[k].at[rows_of(c)], tok[k].at[rows_of(c)], f_send.at[c], chunk_sem(k, c), mates[1],
                sends=even if k == 2 else odd,
            )
            for c in range(CHUNKS)
        ]
        for k in (2, 3)
    ]
    beside = remote(tok_hbm, tok[1], t_send.at[CHUNKS], t_recv.at[2 * CHUNKS], mates[1])

    def norm(k, start, count):
        def body(i, carry):
            at_rows = pl.ds(pl.multiple_of(start + i * 16, 16), 16)
            wide = tok[k][at_rows, :].astype(jnp.float32)
            scale = lax.rsqrt(jnp.sum(wide * wide, axis=-1, keepdims=True) * (1.0 / WIDTH) + 1e-05)
            normed[k][at_rows, :] = (wide * scale * gain_ref[...]).astype(jnp.bfloat16)
            return carry

        lax.fori_loop(0, count // 16, body, 0)

    def do_own(k):
        loads[0].wait()
        norm(0, 0, ROWS)

    def do_beside(k):
        beside.land()
        norm(1, 0, ROWS)

    def do_arrive(k, c):
        crossing[k - 2][c].land()
        handed[k - 2][c].start()
        handed[k - 2][c].landed = True
        if k == 2 and c == CHUNKS - 2:
            for copy in crossing[1]:
                copy.start()
        norm(k, c * PART, PART)

    def rotate(value, at_rows):
        return value * cos_ref[at_rows, :] + pltpu.roll(value, HW // 2, 1) * sin_ref[at_rows, :]

    ready = set()

    def loaded(*which):
        for i in which:
            if i not in ready:
                loads[i].wait()
                ready.add(i)

    def do_kv(k, h):
        loaded(1, 2)
        u = 2 * k + h
        at_rows = slice(h * HALF, (h + 1) * HALF)
        both = jnp.dot(normed[k][at_rows, :], w[:, 0 : 2 * HW], preferred_element_type=jnp.float32)
        kv[u][z, :, 0:HW] = rotate(both[:, 0:HW], at_rows).astype(jnp.bfloat16)
        kv[u][z, :, HW:] = both[:, HW:].astype(jnp.bfloat16)

    def do_q(k):
        loaded(3)
        wide = jnp.dot(normed[k][...], w[:, 2 * HW :], preferred_element_type=jnp.float32)
        for h in range(HEADS):
            qb[k][h * ROWS : (h + 1) * ROWS, :] = rotate(wide[:, h * HW : (h + 1) * HW], slice(0, ROWS)).astype(jnp.bfloat16)

    def ring(buf, k, send, recv):
        hops = {}
        for j in range(1, 5):
            for up in (True, False):
                if j == 4 and up != (k % 2 == 0):
                    continue
                place = lax.rem(z - (j - 1) + RING, RING) if up else lax.rem(z + (j - 1), RING)
                index = k * 7 + (0 if up else 3 + (k % 2 == 0)) + j - 1
                hops[up, j] = remote(
                    buf.at[place], buf.at[place], send.at[index], recv.at[index], z_up if up else z_down
                )
        return hops

    z_hops = [ring(kv[u], u, z_send, z_recv) for u in range(UNITS)]
    vz_hops = [ring(vz[k], k, vz_send, vz_recv) for k in range(DOCS)]

    def step(hops, j):
        for up in (True, False):
            if (up, j - 1) in hops:
                hops[up, j - 1].land()
            if (up, j) in hops:
                hops[up, j].start()

    def do_z(k, h, j):
        step(z_hops[2 * k + h], j)

    def do_vz(k, j):
        step(vz_hops[k], j)

    prevs = [
        remote(kv[u].at[z], prev[u], p_send.at[u], p_recv.at[u], after, sends=gives_prev, takes=takes_prev)
        for u in range(UNITS)
    ]

    def do_prev(k, h):
        prevs[2 * k + h].start()

    offset = [[slash_ref[docs[k], g, t] for t in range(SLOTS)] for k in range(DOCS)]
    vertical = [[vert_ref[docs[k], g, i] for i in range(4)] for k in range(DOCS)]
    mine = [vert_ref[docs[k], g, lax.rem(z, 4)] for k in range(DOCS)]
    shift = [[(offset[k][t] - z + RING - 1) // RING for t in range(SLOTS)] for k in range(DOCS)]

    def turns(k, t):
        steps = lax.rem(shift[k][t], COLS)
        return steps if t < 2 else lax.rem(COLS - steps, COLS)

    y_near = [
        [
            remote(ya[u].at[0, 0:2], ya[u].at[1, 0:2], y_send.at[u * 3], y_recv.at[u * 3], y_up),
            remote(ya[u].at[0, 2:4], ya[u].at[1, 2:4], y_send.at[u * 3 + 1], y_recv.at[u * 3 + 1], y_down),
        ]
        for u in range(UNITS)
    ]
    y_over = [
        remote(yb[u].at[0], yb[u].at[1], y_send.at[u * 3 + 2], y_recv.at[u * 3 + 2], y_far) for u in range(UNITS)
    ]
    x_over = [
        remote(xc[u].at[0], xc[u].at[1], x_send.at[u], x_recv.at[u], x_far, sends=lower, takes=upper)
        for u in range(UNITS)
    ]
    vy_over = [
        [
            remote(vy[k].at[y], vy[k].at[y], vy_send.at[k * 3 + i], vy_recv.at[k * 3 + i], device)
            for i, device in enumerate((y_up, y_far, y_down))
        ]
        for k in range(DOCS)
    ]
    vx_over = [
        remote(vx[k].at[0], vx[k].at[1], vx_send.at[k], vx_recv.at[k], x_far, sends=lower, takes=upper)
        for k in range(DOCS)
    ]

    def do_y1(k, h):
        u = 2 * k + h
        for t in range(SLOTS):
            ya[u][0, t] = kv[u][lax.rem(z - offset[k][t] + LINE, RING)]
        for copy in y_near[u]:
            copy.start()

    def do_y2(k, h):
        u = 2 * k + h
        for copy in y_near[u]:
            copy.land()
        for t in range(SLOTS):
            yb[u][0, t] = ya[u][lax.rem(turns(k, t), 2), t]
        y_over[u].start()

    def do_x1(k, h):
        u = 2 * k + h
        y_over[u].land()
        for t in range(SLOTS):
            xc[u][0, t] = yb[u][turns(k, t) // 2, t]
        x_over[u].start()

    def do_v1(k):
        for h in range(2):

            @pl.when(z // 4 == h)
            def _():
                vy[k][y] = kv[2 * k + h][lax.rem(mine[k], RING)]

        for copy in vy_over[k]:
            copy.start()

    def do_v2(k):
        for copy in vy_over[k]:
            copy.land()
        vx[k][0] = vy[k][lax.rem(mine[k] // RING, COLS)]
        vx_over[k].start()

    def do_v3(k):
        vx_over[k].land()
        vz[k][z] = vx[k][x * (mine[k] < LINE // 2).astype(jnp.int32)]
        do_vz(k, 1)

    def columns(i):
        return pl.ds(pl.multiple_of(g * 512 + i * HW, HW), HW)

    out_own = [
        pltpu.make_async_copy(ob[0].at[i], out_hbm.at[:, columns(i)], local_sem.at[4 + i]) for i in range(HEADS)
    ]

    def out_copy(k, i, receive):
        return remote(
            ob[k].at[i], out_hbm.at[:, columns(i)], o_send.at[(k - 1) * HEADS + i], o_recv.at[receive * HEADS + i],
            mates[k],
        )

    out_sent = [None] + [[out_copy(k, i, 0 if k == 1 else 1 + core) for i in range(HEADS)] for k in range(1, DOCS)]
    out_got = [out_copy(1, i, source) for source in range(3) for i in range(HEADS)]

    low = jnp.float32(-jnp.inf)

    bias = {}

    def do_stage(k):
        for h in range(2):
            u = 2 * k + h
            prevs[u].land()
            x_over[u].land()

            def put(i, value):
                at_rows = slice(i * ROWS + h * HALF, i * ROWS + (h + 1) * HALF)
                kall[at_rows, :] = value[:, 0:HW]
                vall[at_rows, :] = value[:, HW:]

            put(0, kv[u][z])

            @pl.when(z > 0)
            def _():
                put(1, kv[u][lax.rem(z + RING - 1, RING)])

            @pl.when(takes_prev)
            def _():
                put(1, prev[u][...])

            @pl.when(s == 0)
            def _():
                put(1, jnp.zeros((HALF, 2 * HW), jnp.bfloat16))

            for t in range(SLOTS):
                put(2 + t, xc[u][x * (shift[k][t] > y).astype(jnp.int32), t])
            for i in range(4):
                put(2 + SLOTS + i, vz[k][i + 4 * h])
        allowed = [s >= 1] + [s >= offset[k][t] for t in range(SLOTS)]
        for i in range(4):
            good = vertical[k][i] < s - 1
            for t in range(SLOTS):
                good = jnp.logical_and(good, vertical[k][i] != s - offset[k][t])
            allowed.append(good)
        bias[k] = [jnp.where(good, jnp.float32(0.0), low) for good in allowed]

    def do_head(k, i):
        blocks = 2 + SLOTS + 4
        causal = lax.broadcasted_iota(jnp.int32, (ROWS, ROWS), 1) <= lax.broadcasted_iota(jnp.int32, (ROWS, ROWS), 0)
        scores = lax.dot_general(
            qb[k][i * ROWS : (i + 1) * ROWS, :],
            kall[...],
            (((1,), (1,)), ((), ())),
            preferred_element_type=jnp.float32,
        ) * (HW ** (-0.5))
        tiles = [scores[:, n * ROWS : (n + 1) * ROWS] for n in range(blocks)]
        tiles = [jnp.where(causal, tiles[0], low)] + [tiles[n] + bias[k][n - 1] for n in range(1, blocks)]
        highest = tiles[0]
        for tile in tiles[1:]:
            highest = jnp.maximum(highest, tile)
        highest = jnp.max(highest, axis=1, keepdims=True)
        raised = [jnp.exp(tile - highest) for tile in tiles]
        total = raised[0]
        for tile in raised[1:]:
            total = total + tile
        total = jnp.sum(total, axis=1, keepdims=True)
        weights = jnp.concatenate([tile.astype(jnp.bfloat16) for tile in raised], axis=1)
        mixed = jnp.dot(weights, vall[...], preferred_element_type=jnp.float32) / total
        ob[k][i] = mixed.astype(jnp.bfloat16)
        if k == 0:
            out_own[i].start()
        else:
            out_sent[k][i].start()
            out_sent[k][i].landed = True

    for copy in crossing[0]:
        copy.start()
    beside.start()
    does = {
        "own": do_own, "beside": do_beside, "arrive": do_arrive, "kv": do_kv, "q": do_q, "z": do_z, "vz": do_vz,
        "prev": do_prev, "y1": do_y1, "y2": do_y2, "x1": do_x1, "v1": do_v1, "v2": do_v2, "v3": do_v3,
        "stage": do_stage, "head": do_head,
    }
    for name, *which in plan:
        does[name](*which)

    loaded(1, 2, 3)
    for copy in log:
        if not copy.landed:
            copy.land()
        copy.sent()
    for copy in out_own:
        copy.wait()
    for copy in out_got:
        copy.land()


def layer(plan, collective_id, tokens, norm_gain, w_query, key_weight, value_weight, vertical_blocks, slash_offsets):
    cosine, sine = rope_tables(lax.axis_index("seq"))
    bf16 = jnp.bfloat16
    unit = (HALF, 2 * HW)
    dma = pltpu.SemaphoreType.DMA

    def many(shape):
        return [pltpu.VMEM(shape, bf16)] * DOCS

    scratch = (
        many((ROWS, WIDTH))
        + many((ROWS, WIDTH))
        + [pltpu.VMEM((WIDTH, 6 * HW), bf16)]
        + many((RING,) + unit) * 2
        + many(unit) * 2
        + many((2, SLOTS) + unit) * 6
        + many((COLS,) + unit)
        + many((2,) + unit)
        + many((RING,) + unit)
        + many((HEADS * ROWS, HW))
        + [pltpu.VMEM((10 * ROWS, HW), bf16)] * 2
        + many((HEADS, ROWS, HW))
        + [dma((4 + HEADS,)), dma((CHUNKS + 1,)), dma((2 * CHUNKS + 1,)), dma((CHUNKS,))]
    )
    for count in (8, 56, 24, 8, 12, 4, 28, 12):
        scratch += [dma((count,))] * 2
    smem = pl.BlockSpec(memory_space=pltpu.SMEM)
    vmem = pl.BlockSpec(memory_space=pltpu.VMEM)
    hbm = pl.BlockSpec(memory_space=pl.ANY)
    out = pl.pallas_call(
        functools.partial(kernel, plan),
        out_shape=jax.ShapeDtypeStruct((ROWS, DOCS * HEADS * HW), bf16),
        in_specs=[smem, smem, hbm, vmem, hbm, hbm, hbm, vmem, vmem],
        out_specs=hbm,
        scratch_shapes=scratch,
        compiler_params=pltpu.CompilerParams(
            collective_id=collective_id, has_side_effects=True, vmem_limit_bytes=60 * 1024 * 1024
        ),
    )(
        vertical_blocks, slash_offsets, tokens[0], norm_gain[None, :], w_query, key_weight, value_weight, cosine, sine
    )
    return out[None]


IN_SPECS = (
    P("doc", "seq", None),
    P(),
    P(None, "doc"),
    P(None, "doc"),
    P(None, "doc"),
    P(),
    P(),
)


def solution(mesh):
    return jax.shard_map(
        functools.partial(layer, PLAN, 0),
        mesh=mesh,
        in_specs=IN_SPECS,
        out_specs=P("doc", "seq", None),
        check_vma=False,
    )
```

```python
import functools

import jax
import jax.numpy as jnp
from jax import lax
from jax.experimental import pallas as pl
from jax.experimental.pallas import tpu as pltpu
from jax.sharding import PartitionSpec as P

MESH = pl.DeviceIdType.MESH
HEADS = 4
HW = 128
ROWS = 128
HALF = ROWS // 2
WIDTH = 4096
DOCS = 4
UNITS = 2 * DOCS
RING = 8
COLS = 4
SLOTS = 4
CHUNKS = 4
PART = ROWS // CHUNKS
LINE = 64

PLAN = [
    ("own", 0), ("kv", 0, 0), ("z", 0, 0, 1), ("kv", 0, 1), ("z", 0, 1, 1), ("prev", 0, 0), ("prev", 0, 1), ("q", 0),
    ("beside", 1), ("kv", 1, 0), ("z", 1, 0, 1), ("kv", 1, 1), ("z", 1, 1, 1), ("z", 0, 0, 2), ("prev", 1, 0),
    ("prev", 1, 1), ("arrive", 2, 0), ("q", 1), ("z", 0, 1, 2), ("arrive", 2, 1), ("kv", 2, 0), ("z", 2, 0, 1),
    ("prev", 2, 0), ("z", 1, 0, 2), ("arrive", 2, 2), ("z", 1, 1, 2), ("z", 0, 0, 3), ("y1", 0, 0), ("z", 0, 1, 3),
    ("v1", 0), ("y1", 0, 1), ("arrive", 2, 3), ("kv", 2, 1), ("z", 2, 1, 1), ("prev", 2, 1), ("q", 2),
    ("z", 2, 0, 2), ("arrive", 3, 0), ("y2", 0, 0), ("z", 1, 0, 3), ("y1", 1, 0), ("z", 1, 1, 3), ("v1", 1),
    ("y1", 1, 1), ("v2", 0), ("y2", 0, 1), ("arrive", 3, 1), ("kv", 3, 0), ("z", 3, 0, 1), ("z", 2, 1, 2),
    ("prev", 3, 0), ("z", 2, 0, 3), ("y1", 2, 0), ("arrive", 3, 2), ("y2", 1, 0), ("z", 3, 0, 2), ("arrive", 3, 3),
    ("kv", 3, 1), ("z", 3, 1, 1), ("v2", 1), ("prev", 3, 1), ("x1", 0, 0), ("y2", 1, 1), ("q", 3), ("z", 2, 1, 3),
    ("v1", 2), ("y1", 2, 1), ("v3", 0), ("z", 3, 0, 3), ("y1", 3, 0), ("x1", 0, 1), ("v3", 1), ("y2", 2, 0),
    ("z", 3, 1, 2), ("vz", 0, 2), ("x1", 1, 0), ("vz", 1, 2), ("x1", 1, 1), ("z", 3, 1, 3), ("v1", 3), ("y1", 3, 1),
    ("v2", 2), ("vz", 0, 3), ("y2", 2, 1), ("stage", 0), ("head", 0, 0), ("y2", 3, 0), ("vz", 1, 3), ("head", 0, 1),
    ("stage", 1), ("v3", 2), ("x1", 2, 0), ("head", 1, 0), ("v2", 3), ("y2", 3, 1), ("head", 1, 1), ("vz", 2, 2),
    ("x1", 2, 1), ("v3", 3), ("x1", 3, 0), ("vz", 2, 3), ("x1", 3, 1), ("vz", 3, 2), ("stage", 2), ("head", 2, 0),
    ("head", 2, 1), ("vz", 3, 3), ("stage", 3), ("head", 3, 0), ("head", 3, 1),
]


def rope_tables(place):
    positions = place * ROWS + jnp.arange(ROWS, dtype=jnp.int32)
    inverse = jnp.power(jnp.float32(500000.0), -jnp.arange(0, HW, 2, dtype=jnp.float32) / HW)
    angles = positions.astype(jnp.float32)[:, None] * inverse[None, :]
    cosine, sine = jnp.cos(angles), jnp.sin(angles)
    return jnp.concatenate([cosine, cosine], axis=1), jnp.concatenate([-sine, sine], axis=1)


def take(refs, *counts):
    refs = list(refs)
    out = []
    for count in counts:
        out.append(refs[:count] if count > 1 else refs[0])
        del refs[:count]
    return out


def guarded(condition, act):
    if condition is None:
        act()
    else:
        pl.when(condition)(act)


class Copy:
    def __init__(self, log, src, dst, send, recv, device, sends=None, takes=None):
        self.log, self.parts = log, (src, dst, send, recv, device)
        self.sends, self.takes = sends, takes
        self.landed = False

    def make(self):
        src, dst, send, recv, device = self.parts
        return pltpu.make_async_remote_copy(
            src_ref=src, dst_ref=dst, send_sem=send, recv_sem=recv, device_id=device, device_id_type=MESH
        )

    def start(self):
        guarded(self.sends, lambda: self.make().start())
        self.log.append(self)

    def land(self):
        guarded(self.takes, lambda: self.make().wait_recv())
        self.landed = True

    def sent(self):
        guarded(self.sends, lambda: self.make().wait_send())


def kernel(plan, vert_ref, slash_ref, tok_hbm, gain_ref, wq_hbm, wk_hbm, wv_hbm, cos_ref, sin_ref, out_hbm, *scratch):
    (
        tok, normed, w, kv, prev, ya, yb, xc, vy, vx, vz, qb, kall, vall, ob,
        local_sem, t_send, t_recv, f_send, p_send, p_recv, z_send, z_recv, y_send, y_recv,
        x_send, x_recv, vy_send, vy_recv, vx_send, vx_recv, vz_send, vz_recv, o_send, o_recv,
    ) = take(scratch, 4, 4, 1, 8, 8, 8, 8, 8, 4, 4, 4, 4, 1, 1, 4, *([1] * 20))
    s = lax.axis_index("seq")
    g = lax.axis_index("doc")
    core = lax.rem(g, 2)
    z = lax.rem(s, RING)
    row = s // RING
    y = lax.rem(row, COLS)
    x = row // COLS
    across = lax.rem(g - core + 2, 4)
    docs = [g, g + 1 - 2 * core, across, across + 1]

    def at(seq, doc):
        return {"seq": seq, "doc": doc}

    z_up = at(s - z + lax.rem(z + 1, RING), g)
    z_down = at(s - z + lax.rem(z + RING - 1, RING), g)
    z_up_two = at(s - z + lax.rem(z + 2, RING), g)
    z_down_two = at(s - z + lax.rem(z + RING - 2, RING), g)
    y_up = at(s - y * RING + lax.rem(y + 1, COLS) * RING, g)
    y_far = at(s - y * RING + lax.rem(y + 2, COLS) * RING, g)
    y_down = at(s - y * RING + lax.rem(y + 3, COLS) * RING, g)
    x_far = at(lax.rem(s + LINE // 2, LINE), g)
    after = at(lax.rem(s + 1, LINE), g)
    before = at(lax.rem(s + LINE - 1, LINE), g)
    mates = [at(s, doc) for doc in docs]
    peer = at(s, across + core)

    log = []

    def remote(*parts, **ends):
        return Copy(log, *parts, **ends)

    loads = [
        pltpu.make_async_copy(tok_hbm, tok[0], local_sem.at[0]),
        pltpu.make_async_copy(wk_hbm, w.at[:, 0:HW], local_sem.at[1]),
        pltpu.make_async_copy(wv_hbm, w.at[:, HW : 2 * HW], local_sem.at[2]),
        pltpu.make_async_copy(wq_hbm, w.at[:, 2 * HW :], local_sem.at[3]),
    ]
    for load in loads:
        load.start()

    barrier = pltpu.get_barrier_semaphore()
    greeted = mates[1:] + [z_up, z_down, z_up_two, z_down_two, y_up, y_far, y_down, x_far, after, before]
    for device in greeted:
        pl.semaphore_signal(barrier, inc=1, device_id=device, device_id_type=MESH)
    pl.semaphore_wait(barrier, len(greeted))

    even, odd = core == 0, core == 1
    lower, upper = x == 0, x == 1
    gives_prev = jnp.logical_and(z == RING - 1, s < LINE - 1)
    takes_prev = jnp.logical_and(z == 0, s > 0)

    def rows_of(c):
        return pl.ds(c * PART, PART)

    def chunk_sem(k, c):
        return t_recv.at[(k - 2) * CHUNKS + c]

    crossing = [
        [
            remote(
                tok_hbm.at[rows_of(c)], tok[k].at[rows_of(c)], t_send.at[c], chunk_sem(k, c), peer,
                sends=even if k == 2 else odd,
            )
            for c in range(CHUNKS)
        ]
        for k in (2, 3)
    ]
    handed = [
        [
            remote(
                tok[k].at[rows_of(c)], tok[k].at[rows_of(c)], f_send.at[c], chunk_sem(k, c), mates[1],
                sends=even if k == 2 else odd,
            )
            for c in range(CHUNKS)
        ]
        for k in (2, 3)
    ]
    beside = remote(tok_hbm, tok[1], t_send.at[CHUNKS], t_recv.at[2 * CHUNKS], mates[1])

    def norm(k, start, count):
        def body(i, carry):
            at_rows = pl.ds(pl.multiple_of(start + i * 16, 16), 16)
            wide = tok[k][at_rows, :].astype(jnp.float32)
            scale = lax.rsqrt(jnp.sum(wide * wide, axis=-1, keepdims=True) * (1.0 / WIDTH) + 1e-05)
            normed[k][at_rows, :] = (wide * scale * gain_ref[...]).astype(jnp.bfloat16)
            return carry

        lax.fori_loop(0, count // 16, body, 0)

    def do_own(k):
        loads[0].wait()
        norm(0, 0, ROWS)

    def do_beside(k):
        beside.land()
        norm(1, 0, ROWS)

    def do_arrive(k, c):
        crossing[k - 2][c].land()
        handed[k - 2][c].start()
        handed[k - 2][c].landed = True
        if k == 2 and c == CHUNKS - 2:
            for copy in crossing[1]:
                copy.start()
        norm(k, c * PART, PART)

    def rotate(value, at_rows):
        return value * cos_ref[at_rows, :] + pltpu.roll(value, HW // 2, 1) * sin_ref[at_rows, :]

    ready = set()

    def loaded(*which):
        for i in which:
            if i not in ready:
                loads[i].wait()
                ready.add(i)

    def do_kv(k, h):
        loaded(1, 2)
        u = 2 * k + h
        at_rows = slice(h * HALF, (h + 1) * HALF)
        both = jnp.dot(normed[k][at_rows, :], w[:, 0 : 2 * HW], preferred_element_type=jnp.float32)
        kv[u][z, :, 0:HW] = rotate(both[:, 0:HW], at_rows).astype(jnp.bfloat16)
        kv[u][z, :, HW:] = both[:, HW:].astype(jnp.bfloat16)

    def do_q(k):
        loaded(3)
        wide = jnp.dot(normed[k][...], w[:, 2 * HW :], preferred_element_type=jnp.float32)
        for h in range(HEADS):
            qb[k][h * ROWS : (h + 1) * ROWS, :] = rotate(wide[:, h * HW : (h + 1) * HW], slice(0, ROWS)).astype(jnp.bfloat16)

    def ring(buf, k, send, recv):
        behind, ahead = lax.rem(z + RING - 2, RING), lax.rem(z + 2, RING)
        routes = [(z, z_up_two), (z, z_down_two), (z, z_up), (z, z_down)]
        routes += [(behind, z_up_two) if k % 2 == 0 else (ahead, z_down_two), (behind, z_up), (ahead, z_down)]
        return [
            remote(buf.at[place], buf.at[place], send.at[k * 7 + i], recv.at[k * 7 + i], device)
            for i, (place, device) in enumerate(routes)
        ]

    z_hops = [ring(kv[u], u, z_send, z_recv) for u in range(UNITS)]
    vz_hops = [ring(vz[k], k, vz_send, vz_recv) for k in range(DOCS)]

    def step(hops, j):
        lands = ((), (0, 1), (2, 3, 4, 5, 6))[j - 1]
        starts = (range(4), range(4, 7), ())[j - 1]
        for i in lands:
            hops[i].land()
        for i in starts:
            hops[i].start()

    def do_z(k, h, j):
        step(z_hops[2 * k + h], j)

    def do_vz(k, j):
        step(vz_hops[k], j)

    prevs = [
        remote(kv[u].at[z], prev[u], p_send.at[u], p_recv.at[u], after, sends=gives_prev, takes=takes_prev)
        for u in range(UNITS)
    ]

    def do_prev(k, h):
        prevs[2 * k + h].start()

    offset = [[slash_ref[docs[k], g, t] for t in range(SLOTS)] for k in range(DOCS)]
    vertical = [[vert_ref[docs[k], g, i] for i in range(4)] for k in range(DOCS)]
    mine = [vert_ref[docs[k], g, lax.rem(z, 4)] for k in range(DOCS)]
    shift = [[(offset[k][t] - z + RING - 1) // RING for t in range(SLOTS)] for k in range(DOCS)]

    def turns(k, t):
        steps = lax.rem(shift[k][t], COLS)
        return steps if t < 2 else lax.rem(COLS - steps, COLS)

    y_near = [
        [
            remote(ya[u].at[0, 0:2], ya[u].at[1, 0:2], y_send.at[u * 3], y_recv.at[u * 3], y_up),
            remote(ya[u].at[0, 2:4], ya[u].at[1, 2:4], y_send.at[u * 3 + 1], y_recv.at[u * 3 + 1], y_down),
        ]
        for u in range(UNITS)
    ]
    y_over = [
        remote(yb[u].at[0], yb[u].at[1], y_send.at[u * 3 + 2], y_recv.at[u * 3 + 2], y_far) for u in range(UNITS)
    ]
    x_over = [
        remote(xc[u].at[0], xc[u].at[1], x_send.at[u], x_recv.at[u], x_far, sends=lower, takes=upper)
        for u in range(UNITS)
    ]
    vy_over = [
        [
            remote(vy[k].at[y], vy[k].at[y], vy_send.at[k * 3 + i], vy_recv.at[k * 3 + i], device)
            for i, device in enumerate((y_up, y_far, y_down))
        ]
        for k in range(DOCS)
    ]
    vx_over = [
        remote(vx[k].at[0], vx[k].at[1], vx_send.at[k], vx_recv.at[k], x_far, sends=lower, takes=upper)
        for k in range(DOCS)
    ]

    def do_y1(k, h):
        u = 2 * k + h
        for t in range(SLOTS):
            ya[u][0, t] = kv[u][lax.rem(z - offset[k][t] + LINE, RING)]
        for copy in y_near[u]:
            copy.start()

    def do_y2(k, h):
        u = 2 * k + h
        for copy in y_near[u]:
            copy.land()
        for t in range(SLOTS):
            yb[u][0, t] = ya[u][lax.rem(turns(k, t), 2), t]
        y_over[u].start()

    def do_x1(k, h):
        u = 2 * k + h
        y_over[u].land()
        for t in range(SLOTS):
            xc[u][0, t] = yb[u][turns(k, t) // 2, t]
        x_over[u].start()

    def do_v1(k):
        for h in range(2):

            @pl.when(z // 4 == h)
            def _():
                vy[k][y] = kv[2 * k + h][lax.rem(mine[k], RING)]

        for copy in vy_over[k]:
            copy.start()

    def do_v2(k):
        for copy in vy_over[k]:
            copy.land()
        vx[k][0] = vy[k][lax.rem(mine[k] // RING, COLS)]
        vx_over[k].start()

    def do_v3(k):
        vx_over[k].land()
        vz[k][z] = vx[k][x * (mine[k] < LINE // 2).astype(jnp.int32)]
        do_vz(k, 1)

    def columns(i):
        return pl.ds(pl.multiple_of(g * 512 + i * HW, HW), HW)

    out_own = [
        pltpu.make_async_copy(ob[0].at[i], out_hbm.at[:, columns(i)], local_sem.at[4 + i]) for i in range(HEADS)
    ]

    def out_copy(k, i, receive):
        return remote(
            ob[k].at[i], out_hbm.at[:, columns(i)], o_send.at[(k - 1) * HEADS + i], o_recv.at[receive * HEADS + i],
            mates[k],
        )

    out_sent = [None] + [[out_copy(k, i, 0 if k == 1 else 1 + core) for i in range(HEADS)] for k in range(1, DOCS)]
    out_got = [out_copy(1, i, source) for source in range(3) for i in range(HEADS)]

    low = jnp.float32(-jnp.inf)

    bias = {}

    def do_stage(k):
        for h in range(2):
            u = 2 * k + h
            prevs[u].land()
            x_over[u].land()

            def put(i, value):
                at_rows = slice(i * ROWS + h * HALF, i * ROWS + (h + 1) * HALF)
                kall[at_rows, :] = value[:, 0:HW]
                vall[at_rows, :] = value[:, HW:]

            put(0, kv[u][z])

            @pl.when(z > 0)
            def _():
                put(1, kv[u][lax.rem(z + RING - 1, RING)])

            @pl.when(takes_prev)
            def _():
                put(1, prev[u][...])

            @pl.when(s == 0)
            def _():
                put(1, jnp.zeros((HALF, 2 * HW), jnp.bfloat16))

            for t in range(SLOTS):
                put(2 + t, xc[u][x * (shift[k][t] > y).astype(jnp.int32), t])
            for i in range(4):
                put(2 + SLOTS + i, vz[k][i + 4 * h])
        allowed = [s >= 1] + [s >= offset[k][t] for t in range(SLOTS)]
        for i in range(4):
            good = vertical[k][i] < s - 1
            for t in range(SLOTS):
                good = jnp.logical_and(good, vertical[k][i] != s - offset[k][t])
            allowed.append(good)
        bias[k] = [jnp.where(good, jnp.float32(0.0), low) for good in allowed]

    def do_head(k, pair):
        blocks = 2 + SLOTS + 4
        causal = lax.broadcasted_iota(jnp.int32, (ROWS, ROWS), 1) <= lax.broadcasted_iota(jnp.int32, (ROWS, ROWS), 0)
        for i in (2 * pair, 2 * pair + 1):
            scores = lax.dot_general(
                qb[k][i * ROWS : (i + 1) * ROWS, :],
                kall[...],
                (((1,), (1,)), ((), ())),
                preferred_element_type=jnp.float32,
            )
            tiles = [scores[:, n * ROWS : (n + 1) * ROWS] for n in range(blocks)]
            tiles = [jnp.where(causal, tiles[0], low)] + [tiles[n] + bias[k][n - 1] for n in range(1, blocks)]
            highest = tiles[0]
            for tile in tiles[1:]:
                highest = jnp.maximum(highest, tile)
            highest = jnp.max(highest, axis=1, keepdims=True)
            raised = [jnp.exp2((tile - highest) * (HW ** (-0.5) * 1.4426950408889634)) for tile in tiles]
            total = raised[0]
            for tile in raised[1:]:
                total = total + tile
            total = jnp.sum(total, axis=1, keepdims=True)
            weights = jnp.concatenate([tile.astype(jnp.bfloat16) for tile in raised], axis=1)
            mixed = jnp.dot(weights, vall[...], preferred_element_type=jnp.float32) / total
            ob[k][i] = mixed.astype(jnp.bfloat16)
            if k == 0:
                out_own[i].start()
            else:
                out_sent[k][i].start()
                out_sent[k][i].landed = True

    for copy in crossing[0]:
        copy.start()
    beside.start()
    does = {
        "own": do_own, "beside": do_beside, "arrive": do_arrive, "kv": do_kv, "q": do_q, "z": do_z, "vz": do_vz,
        "prev": do_prev, "y1": do_y1, "y2": do_y2, "x1": do_x1, "v1": do_v1, "v2": do_v2, "v3": do_v3,
        "stage": do_stage, "head": do_head,
    }
    for name, *which in plan:
        does[name](*which)

    loaded(1, 2, 3)
    for copy in log:
        if not copy.landed:
            copy.land()
        copy.sent()
    for copy in out_own:
        copy.wait()
    for copy in out_got:
        copy.land()


def layer(plan, collective_id, tokens, norm_gain, w_query, key_weight, value_weight, vertical_blocks, slash_offsets):
    cosine, sine = rope_tables(lax.axis_index("seq"))
    bf16 = jnp.bfloat16
    unit = (HALF, 2 * HW)
    dma = pltpu.SemaphoreType.DMA

    def many(shape):
        return [pltpu.VMEM(shape, bf16)] * DOCS

    scratch = (
        many((ROWS, WIDTH))
        + many((ROWS, WIDTH))
        + [pltpu.VMEM((WIDTH, 6 * HW), bf16)]
        + many((RING,) + unit) * 2
        + many(unit) * 2
        + many((2, SLOTS) + unit) * 6
        + many((COLS,) + unit)
        + many((2,) + unit)
        + many((RING,) + unit)
        + many((HEADS * ROWS, HW))
        + [pltpu.VMEM((10 * ROWS, HW), bf16)] * 2
        + many((HEADS, ROWS, HW))
        + [dma((4 + HEADS,)), dma((CHUNKS + 1,)), dma((2 * CHUNKS + 1,)), dma((CHUNKS,))]
    )
    for count in (8, 56, 24, 8, 12, 4, 28, 12):
        scratch += [dma((count,))] * 2
    smem = pl.BlockSpec(memory_space=pltpu.SMEM)
    vmem = pl.BlockSpec(memory_space=pltpu.VMEM)
    hbm = pl.BlockSpec(memory_space=pl.ANY)
    out = pl.pallas_call(
        functools.partial(kernel, plan),
        out_shape=jax.ShapeDtypeStruct((ROWS, DOCS * HEADS * HW), bf16),
        in_specs=[smem, smem, hbm, vmem, hbm, hbm, hbm, vmem, vmem],
        out_specs=hbm,
        scratch_shapes=scratch,
        compiler_params=pltpu.CompilerParams(
            collective_id=collective_id, has_side_effects=True, vmem_limit_bytes=60 * 1024 * 1024
        ),
    )(
        vertical_blocks, slash_offsets, tokens[0], norm_gain[None, :], w_query, key_weight, value_weight, cosine, sine
    )
    return out[None]


IN_SPECS = (
    P("doc", "seq", None),
    P(),
    P(None, "doc"),
    P(None, "doc"),
    P(None, "doc"),
    P(),
    P(),
)


def solution(mesh):
    return jax.shard_map(
        functools.partial(layer, PLAN, 0),
        mesh=mesh,
        in_specs=IN_SPECS,
        out_specs=P("doc", "seq", None),
        check_vma=False,
    )
```

```python
import functools

import jax
import jax.numpy as jnp
import numpy as np
from jax import lax
from jax.experimental import pallas as pl
from jax.experimental.pallas import tpu as pltpu
from jax.sharding import PartitionSpec as P

MESH = pl.DeviceIdType.MESH
HEADS = 4
HW = 128
ROWS = 128
HALF = ROWS // 2
WIDTH = 4096
DOCS = 4
UNITS = 2 * DOCS
RING = 8
COLS = 4
SLOTS = 4
CHUNKS = 4
PART = ROWS // CHUNKS
LINE = 64

PLAN = [
    ("own", 0), ("kv", 0, 0), ("kv", 0, 1), ("z", 0, 0, 1), ("z", 0, 1, 1), ("prev", 0, 0), ("prev", 0, 1), ("q", 0),
    ("beside", 1), ("kv", 1, 0), ("kv", 1, 1), ("prev", 1, 0), ("prev", 1, 1), ("arrive", 2, 0), ("z", 0, 0, 2),
    ("z", 1, 0, 1), ("q", 1), ("z", 0, 1, 2), ("z", 1, 1, 1), ("arrive", 2, 1), ("kv", 2, 0), ("z", 2, 0, 1),
    ("prev", 2, 0), ("z", 0, 0, 3), ("y1", 0, 0), ("arrive", 2, 2), ("z", 1, 0, 2), ("z", 0, 1, 3), ("v1", 0),
    ("y1", 0, 1), ("arrive", 2, 3), ("kv", 2, 1), ("y2", 0, 0), ("z", 1, 1, 2), ("z", 2, 1, 1), ("prev", 2, 1),
    ("q", 2), ("z", 2, 0, 2), ("arrive", 3, 0), ("v2", 0), ("y2", 0, 1), ("z", 1, 0, 3), ("y1", 1, 0),
    ("z", 1, 1, 3), ("v1", 1), ("y1", 1, 1), ("arrive", 3, 1), ("kv", 3, 0), ("z", 3, 0, 1), ("prev", 3, 0),
    ("z", 2, 1, 2), ("arrive", 3, 2), ("z", 2, 0, 3), ("y1", 2, 0), ("y2", 1, 0), ("z", 3, 0, 2), ("arrive", 3, 3),
    ("kv", 3, 1), ("x1", 0, 0), ("x1", 0, 1), ("z", 3, 1, 1), ("v2", 1), ("prev", 3, 1), ("q", 3), ("y2", 1, 1),
    ("z", 2, 1, 3), ("v1", 2), ("y1", 2, 1), ("v3", 0), ("y2", 2, 0), ("z", 3, 0, 3), ("y1", 3, 0), ("z", 3, 1, 2),
    ("x1", 1, 0), ("vz", 0, 2), ("x1", 1, 1), ("v3", 1), ("v2", 2), ("z", 3, 1, 3), ("v1", 3), ("y1", 3, 1),
    ("y2", 2, 1), ("vz", 0, 3), ("stage", 0), ("head", 0, 0), ("x1", 2, 0), ("vz", 1, 2), ("y2", 3, 0),
    ("head", 0, 1), ("v3", 2), ("v2", 3), ("y2", 3, 1), ("vz", 1, 3), ("stage", 1), ("head", 1, 0), ("x1", 2, 1),
    ("v3", 3), ("vz", 2, 2), ("head", 1, 1), ("x1", 3, 0), ("vz", 3, 2), ("x1", 3, 1), ("vz", 2, 3), ("stage", 2),
    ("head", 2, 0), ("head", 2, 1), ("vz", 3, 3), ("stage", 3), ("head", 3, 0), ("head", 3, 1),
]


def rope_constants():
    inverse = 500000.0 ** (-np.arange(0, HW, 2, dtype=np.float64) / HW)
    inverse = np.concatenate([inverse, inverse]).astype(np.float32).astype(np.float64)[None, :]
    near = np.arange(ROWS, dtype=np.float64)[:, None] * inverse
    far = np.arange(LINE, dtype=np.float64)[:, None] * ROWS * inverse
    return [jnp.asarray(f(angle), jnp.float32) for angle in (near, far) for f in (np.cos, np.sin)]


def take(refs, *counts):
    refs = list(refs)
    out = []
    for count in counts:
        out.append(refs[:count] if count > 1 else refs[0])
        del refs[:count]
    return out


def guarded(condition, act):
    if condition is None:
        act()
    else:
        pl.when(condition)(act)


class Copy:
    def __init__(self, log, src, dst, send, recv, device, sends=None, takes=None):
        self.log, self.parts = log, (src, dst, send, recv, device)
        self.sends, self.takes = sends, takes
        self.landed = False

    def make(self):
        src, dst, send, recv, device = self.parts
        return pltpu.make_async_remote_copy(
            src_ref=src, dst_ref=dst, send_sem=send, recv_sem=recv, device_id=device, device_id_type=MESH
        )

    def start(self):
        guarded(self.sends, lambda: self.make().start())
        self.log.append(self)

    def land(self):
        guarded(self.takes, lambda: self.make().wait_recv())
        self.landed = True

    def sent(self):
        guarded(self.sends, lambda: self.make().wait_send())


def kernel(plan, vert_ref, slash_ref, tok_hbm, gain_ref, wq_hbm, wk_hbm, wv_hbm, near_cos, near_sin, far_cos, far_sin, out_ref, *scratch):
    (
        tok, normed, w, kv, prev, ya, yb, xc, vy, vx, vz, qb, kall, vall, ob, cos_ref, sin_ref,
        local_sem, t_send, t_recv, f_send, p_send, p_recv, z_send, z_recv, y_send, y_recv,
        x_send, x_recv, vy_send, vy_recv, vx_send, vx_recv, vz_send, vz_recv, o_send, o_recv,
    ) = take(scratch, 4, 4, 1, 8, 8, 8, 8, 8, 4, 4, 4, 4, 1, 1, 4, 1, 1, *([1] * 20))
    s = lax.axis_index("seq")
    g = lax.axis_index("doc")
    core = lax.rem(g, 2)
    z = lax.rem(s, RING)
    row = s // RING
    y = lax.rem(row, COLS)
    x = row // COLS
    across = lax.rem(g - core + 2, 4)
    docs = [g, g + 1 - 2 * core, across, across + 1]

    def at(seq, doc):
        return {"seq": seq, "doc": doc}

    z_up = at(s - z + lax.rem(z + 1, RING), g)
    z_down = at(s - z + lax.rem(z + RING - 1, RING), g)
    z_up_two = at(s - z + lax.rem(z + 2, RING), g)
    z_down_two = at(s - z + lax.rem(z + RING - 2, RING), g)
    y_up = at(s - y * RING + lax.rem(y + 1, COLS) * RING, g)
    y_far = at(s - y * RING + lax.rem(y + 2, COLS) * RING, g)
    y_down = at(s - y * RING + lax.rem(y + 3, COLS) * RING, g)
    x_far = at(lax.rem(s + LINE // 2, LINE), g)
    after = at(lax.rem(s + 1, LINE), g)
    before = at(lax.rem(s + LINE - 1, LINE), g)
    mates = [at(s, doc) for doc in docs]
    peer = at(s, across + core)

    log = []

    def remote(*parts, **ends):
        return Copy(log, *parts, **ends)

    loads = [
        pltpu.make_async_copy(tok_hbm, tok[0], local_sem.at[0]),
        pltpu.make_async_copy(wk_hbm, w.at[:, 0:HW], local_sem.at[1]),
        pltpu.make_async_copy(wv_hbm, w.at[:, HW : 2 * HW], local_sem.at[2]),
        pltpu.make_async_copy(wq_hbm, w.at[:, 2 * HW :], local_sem.at[3]),
    ]
    for load in loads:
        load.start()

    barrier = pltpu.get_barrier_semaphore()
    greeted = mates[1:] + [z_up, z_down, z_up_two, z_down_two, y_up, y_far, y_down, x_far, after, before]
    for device in greeted:
        pl.semaphore_signal(barrier, inc=1, device_id=device, device_id_type=MESH)
    pl.semaphore_wait(barrier, len(greeted))

    even, odd = core == 0, core == 1
    lower, upper = x == 0, x == 1
    gives_prev = jnp.logical_and(z == RING - 1, s < LINE - 1)
    takes_prev = jnp.logical_and(z == 0, s > 0)

    def rows_of(c):
        return pl.ds(c * PART, PART)

    def chunk_sem(k, c):
        return t_recv.at[(k - 2) * CHUNKS + c]

    crossing = [
        [
            remote(
                tok_hbm.at[rows_of(c)], tok[k].at[rows_of(c)], t_send.at[c], chunk_sem(k, c), peer,
                sends=even if k == 2 else odd,
            )
            for c in range(CHUNKS)
        ]
        for k in (2, 3)
    ]
    handed = [
        [
            remote(
                tok[k].at[rows_of(c)], tok[k].at[rows_of(c)], f_send.at[c], chunk_sem(k, c), mates[1],
                sends=even if k == 2 else odd,
            )
            for c in range(CHUNKS)
        ]
        for k in (2, 3)
    ]
    beside = remote(tok_hbm, tok[1], t_send.at[CHUNKS], t_recv.at[2 * CHUNKS], mates[1])

    def norm(k, start, count):
        def body(i, carry):
            at_rows = pl.ds(pl.multiple_of(start + i * 16, 16), 16)
            wide = tok[k][at_rows, :].astype(jnp.float32)
            scale = lax.rsqrt(jnp.sum(wide * wide, axis=-1, keepdims=True) * (1.0 / WIDTH) + 1e-05)
            normed[k][at_rows, :] = (wide * scale * gain_ref[...]).astype(jnp.bfloat16)
            return carry

        lax.fori_loop(0, count // 16, body, 0)

    def do_own(k):
        turn_cos, turn_sin = far_cos[pl.ds(s, 1), :], far_sin[pl.ds(s, 1), :]
        sign = jnp.where(lax.broadcasted_iota(jnp.int32, (1, HW), 1) < HW // 2, -1.0, 1.0)
        cos_ref[...] = near_cos[...] * turn_cos - near_sin[...] * turn_sin
        sin_ref[...] = (near_sin[...] * turn_cos + near_cos[...] * turn_sin) * sign
        loads[0].wait()
        norm(0, 0, ROWS)

    def do_beside(k):
        beside.land()
        norm(1, 0, ROWS)

    def do_arrive(k, c):
        crossing[k - 2][c].land()
        handed[k - 2][c].start()
        handed[k - 2][c].landed = True
        if k == 2 and c == CHUNKS - 2:
            for copy in crossing[1]:
                copy.start()
        norm(k, c * PART, PART)

    def rotate(value, at_rows):
        return value * cos_ref[at_rows, :] + pltpu.roll(value, HW // 2, 1) * sin_ref[at_rows, :]

    ready = set()

    def loaded(*which):
        for i in which:
            if i not in ready:
                loads[i].wait()
                ready.add(i)

    def do_kv(k, h):
        loaded(1, 2)
        u = 2 * k + h
        at_rows = slice(h * HALF, (h + 1) * HALF)
        both = jnp.dot(normed[k][at_rows, :], w[:, 0 : 2 * HW], preferred_element_type=jnp.float32)
        kv[u][z, :, 0:HW] = rotate(both[:, 0:HW], at_rows).astype(jnp.bfloat16)
        kv[u][z, :, HW:] = both[:, HW:].astype(jnp.bfloat16)

    def do_q(k):
        loaded(3)
        wide = jnp.dot(normed[k][...], w[:, 2 * HW :], preferred_element_type=jnp.float32)
        for h in range(HEADS):
            qb[k][h * ROWS : (h + 1) * ROWS, :] = rotate(wide[:, h * HW : (h + 1) * HW], slice(0, ROWS)).astype(jnp.bfloat16)

    def ring(buf, k, send, recv):
        behind, ahead = lax.rem(z + RING - 2, RING), lax.rem(z + 2, RING)
        routes = [(z, z_up_two), (z, z_down_two), (z, z_up), (z, z_down)]
        routes += [(behind, z_up_two) if k % 2 == 0 else (ahead, z_down_two), (behind, z_up), (ahead, z_down)]
        return [
            remote(buf.at[place], buf.at[place], send.at[k * 7 + i], recv.at[k * 7 + i], device)
            for i, (place, device) in enumerate(routes)
        ]

    z_hops = [ring(kv[u], u, z_send, z_recv) for u in range(UNITS)]
    vz_hops = [ring(vz[k], k, vz_send, vz_recv) for k in range(DOCS)]

    def step(hops, j):
        lands = ((), (0, 1), (2, 3, 4, 5, 6))[j - 1]
        starts = (range(4), range(4, 7), ())[j - 1]
        for i in lands:
            hops[i].land()
        for i in starts:
            hops[i].start()

    def do_z(k, h, j):
        step(z_hops[2 * k + h], j)

    def do_vz(k, j):
        step(vz_hops[k], j)

    prevs = [
        remote(kv[u].at[z], prev[u], p_send.at[u], p_recv.at[u], after, sends=gives_prev, takes=takes_prev)
        for u in range(UNITS)
    ]

    def do_prev(k, h):
        prevs[2 * k + h].start()

    offset = [[slash_ref[docs[k], g, t] for t in range(SLOTS)] for k in range(DOCS)]
    vertical = [[vert_ref[docs[k], g, i] for i in range(4)] for k in range(DOCS)]
    mine = [vert_ref[docs[k], g, lax.rem(z, 4)] for k in range(DOCS)]
    shift = [[(offset[k][t] - z + RING - 1) // RING for t in range(SLOTS)] for k in range(DOCS)]

    def turns(k, t):
        steps = lax.rem(shift[k][t], COLS)
        return steps if t < 2 else lax.rem(COLS - steps, COLS)

    y_near = [
        [
            remote(ya[u].at[0, 0:2], ya[u].at[1, 0:2], y_send.at[u * 3], y_recv.at[u * 3], y_up),
            remote(ya[u].at[0, 2:4], ya[u].at[1, 2:4], y_send.at[u * 3 + 1], y_recv.at[u * 3 + 1], y_down),
        ]
        for u in range(UNITS)
    ]
    y_over = [
        remote(yb[u].at[0], yb[u].at[1], y_send.at[u * 3 + 2], y_recv.at[u * 3 + 2], y_far) for u in range(UNITS)
    ]
    x_over = [
        remote(xc[u].at[0], xc[u].at[1], x_send.at[u], x_recv.at[u], x_far, sends=lower, takes=upper)
        for u in range(UNITS)
    ]
    vy_over = [
        [
            remote(vy[k].at[y], vy[k].at[y], vy_send.at[k * 3 + i], vy_recv.at[k * 3 + i], device)
            for i, device in enumerate((y_up, y_far, y_down))
        ]
        for k in range(DOCS)
    ]
    vx_over = [
        remote(vx[k].at[0], vx[k].at[1], vx_send.at[k], vx_recv.at[k], x_far, sends=lower, takes=upper)
        for k in range(DOCS)
    ]

    def do_y1(k, h):
        u = 2 * k + h
        for t in range(SLOTS):
            ya[u][0, t] = kv[u][lax.rem(z - offset[k][t] + LINE, RING)]
        for copy in y_near[u]:
            copy.start()

    def do_y2(k, h):
        u = 2 * k + h
        for copy in y_near[u]:
            copy.land()
        for t in range(SLOTS):
            yb[u][0, t] = ya[u][lax.rem(turns(k, t), 2), t]
        y_over[u].start()

    def do_x1(k, h):
        u = 2 * k + h
        y_over[u].land()
        for t in range(SLOTS):
            xc[u][0, t] = yb[u][turns(k, t) // 2, t]
        x_over[u].start()

    def do_v1(k):
        for h in range(2):

            @pl.when(z // 4 == h)
            def _():
                vy[k][y] = kv[2 * k + h][lax.rem(mine[k], RING)]

        for copy in vy_over[k]:
            copy.start()

    def do_v2(k):
        for copy in vy_over[k]:
            copy.land()
        vx[k][0] = vy[k][lax.rem(mine[k] // RING, COLS)]
        vx_over[k].start()

    def do_v3(k):
        vx_over[k].land()
        vz[k][z] = vx[k][x * (mine[k] < LINE // 2).astype(jnp.int32)]
        do_vz(k, 1)

    def columns(i):
        return pl.ds(pl.multiple_of(g * 512 + i * HW, HW), HW)

    out_own = [
        pltpu.make_async_copy(ob[0].at[i], out_ref.at[:, columns(i)], local_sem.at[4 + i]) for i in range(HEADS)
    ]

    def out_copy(k, i, receive):
        return remote(
            ob[k].at[i], out_ref.at[:, columns(i)], o_send.at[(k - 1) * HEADS + i], o_recv.at[receive * HEADS + i],
            mates[k],
        )

    out_sent = [None] + [[out_copy(k, i, 0 if k == 1 else 1 + core) for i in range(HEADS)] for k in range(1, DOCS)]
    out_got = [out_copy(1, i, source) for source in range(3) for i in range(HEADS)]

    low = jnp.float32(-jnp.inf)

    bias = {}

    def do_stage(k):
        for h in range(2):
            u = 2 * k + h
            prevs[u].land()
            x_over[u].land()

            def put(i, value):
                at_rows = slice(i * ROWS + h * HALF, i * ROWS + (h + 1) * HALF)
                kall[at_rows, :] = value[:, 0:HW]
                vall[at_rows, :] = value[:, HW:]

            put(0, kv[u][z])

            @pl.when(z > 0)
            def _():
                put(1, kv[u][lax.rem(z + RING - 1, RING)])

            @pl.when(takes_prev)
            def _():
                put(1, prev[u][...])

            @pl.when(s == 0)
            def _():
                put(1, jnp.zeros((HALF, 2 * HW), jnp.bfloat16))

            for t in range(SLOTS):
                put(2 + t, xc[u][x * (shift[k][t] > y).astype(jnp.int32), t])
            for i in range(4):
                put(2 + SLOTS + i, vz[k][i + 4 * h])
        allowed = [s >= 1] + [s >= offset[k][t] for t in range(SLOTS)]
        for i in range(4):
            good = vertical[k][i] < s - 1
            for t in range(SLOTS):
                good = jnp.logical_and(good, vertical[k][i] != s - offset[k][t])
            allowed.append(good)
        bias[k] = [jnp.where(good, jnp.float32(0.0), low) for good in allowed]

    def do_head(k, pair):
        blocks = 2 + SLOTS + 4
        causal = lax.broadcasted_iota(jnp.int32, (ROWS, ROWS), 1) <= lax.broadcasted_iota(jnp.int32, (ROWS, ROWS), 0)
        for i in (2 * pair, 2 * pair + 1):
            scores = lax.dot_general(
                qb[k][i * ROWS : (i + 1) * ROWS, :],
                kall[...],
                (((1,), (1,)), ((), ())),
                preferred_element_type=jnp.float32,
            )
            tiles = [scores[:, n * ROWS : (n + 1) * ROWS] for n in range(blocks)]
            tiles = [jnp.where(causal, tiles[0], low)] + [tiles[n] + bias[k][n - 1] for n in range(1, blocks)]
            highest = tiles[0]
            for tile in tiles[1:]:
                highest = jnp.maximum(highest, tile)
            highest = jnp.max(highest, axis=1, keepdims=True)
            raised = [jnp.exp2((tile - highest) * (HW ** (-0.5) * 1.4426950408889634)) for tile in tiles]
            total = raised[0]
            for tile in raised[1:]:
                total = total + tile
            total = jnp.sum(total, axis=1, keepdims=True)
            weights = jnp.concatenate([tile.astype(jnp.bfloat16) for tile in raised], axis=1)
            mixed = jnp.dot(weights, vall[...], preferred_element_type=jnp.float32) / total
            ob[k][i] = mixed.astype(jnp.bfloat16)
            if k == 0:
                out_own[i].start()
            else:
                out_sent[k][i].start()
                out_sent[k][i].landed = True

    for copy in crossing[0]:
        copy.start()
    beside.start()
    does = {
        "own": do_own, "beside": do_beside, "arrive": do_arrive, "kv": do_kv, "q": do_q, "z": do_z, "vz": do_vz,
        "prev": do_prev, "y1": do_y1, "y2": do_y2, "x1": do_x1, "v1": do_v1, "v2": do_v2, "v3": do_v3,
        "stage": do_stage, "head": do_head,
    }
    for name, *which in plan:
        does[name](*which)

    loaded(1, 2, 3)
    for copy in log:
        if not copy.landed:
            copy.land()
        copy.sent()
    for copy in out_own:
        copy.wait()
    for copy in out_got:
        copy.land()


def layer(plan, collective_id, tokens, norm_gain, w_query, key_weight, value_weight, vertical_blocks, slash_offsets):
    bf16 = jnp.bfloat16
    unit = (HALF, 2 * HW)
    dma = pltpu.SemaphoreType.DMA

    def many(shape):
        return [pltpu.VMEM(shape, bf16)] * DOCS

    scratch = (
        many((ROWS, WIDTH))
        + many((ROWS, WIDTH))
        + [pltpu.VMEM((WIDTH, 6 * HW), bf16)]
        + many((RING,) + unit) * 2
        + many(unit) * 2
        + many((2, SLOTS) + unit) * 6
        + many((COLS,) + unit)
        + many((2,) + unit)
        + many((RING,) + unit)
        + many((HEADS * ROWS, HW))
        + [pltpu.VMEM((10 * ROWS, HW), bf16)] * 2
        + many((HEADS, ROWS, HW))
        + [pltpu.VMEM((ROWS, HW), jnp.float32)] * 2
        + [dma((4 + HEADS,)), dma((CHUNKS + 1,)), dma((2 * CHUNKS + 1,)), dma((CHUNKS,))]
    )
    for count in (8, 56, 24, 8, 12, 4, 28, 12):
        scratch += [dma((count,))] * 2
    smem = pl.BlockSpec(memory_space=pltpu.SMEM)
    vmem = pl.BlockSpec(memory_space=pltpu.VMEM)
    hbm = pl.BlockSpec(memory_space=pl.ANY)
    out = pl.pallas_call(
        functools.partial(kernel, plan),
        out_shape=pltpu.VMEM((ROWS, DOCS * HEADS * HW), bf16),
        in_specs=[smem, smem, hbm, vmem, hbm, hbm, hbm] + [vmem] * 4,
        out_specs=vmem,
        scratch_shapes=scratch,
        compiler_params=pltpu.CompilerParams(
            collective_id=collective_id, has_side_effects=True, vmem_limit_bytes=60 * 1024 * 1024
        ),
    )(
        vertical_blocks,
        slash_offsets,
        tokens[0],
        norm_gain[None, :],
        w_query,
        key_weight,
        value_weight,
        *rope_constants(),
    )
    return out[None]


IN_SPECS = (
    P("doc", "seq", None),
    P(),
    P(None, "doc"),
    P(None, "doc"),
    P(None, "doc"),
    P(),
    P(),
)


def solution(mesh):
    return jax.shard_map(
        functools.partial(layer, PLAN, 0),
        mesh=mesh,
        in_specs=IN_SPECS,
        out_specs=P("doc", "seq", None),
        check_vma=False,
    )
```

```python
import functools

import jax
import jax.numpy as jnp
import numpy as np
from jax import lax
from jax.experimental import pallas as pl
from jax.experimental.pallas import tpu as pltpu
from jax.sharding import PartitionSpec as P

MESH = pl.DeviceIdType.MESH
HEADS = 4
HW = 128
ROWS = 128
HALF = ROWS // 2
WIDTH = 4096
DOCS = 4
UNITS = 2 * DOCS
RING = 8
COLS = 4
SLOTS = 4
CHUNKS = 4
PART = ROWS // CHUNKS
LINE = 64

PLAN = [
    ("own", 0), ("kv", 0, 0), ("kv", 0, 1), ("z", 0, 0, 1), ("z", 0, 1, 1), ("prev", 0, 0), ("prev", 0, 1), ("q", 0),
    ("beside", 1), ("kv", 1, 0), ("kv", 1, 1), ("prev", 1, 0), ("prev", 1, 1), ("arrive", 2, 0), ("z", 0, 0, 2),
    ("z", 1, 0, 1), ("q", 1), ("z", 0, 1, 2), ("z", 1, 1, 1), ("arrive", 2, 1), ("kv", 2, 0), ("z", 2, 0, 1),
    ("prev", 2, 0), ("z", 0, 0, 3), ("y1", 0, 0), ("arrive", 2, 2), ("z", 1, 0, 2), ("z", 0, 1, 3), ("v1", 0),
    ("y1", 0, 1), ("arrive", 2, 3), ("kv", 2, 1), ("y2", 0, 0), ("z", 1, 1, 2), ("z", 2, 1, 1), ("prev", 2, 1),
    ("q", 2), ("z", 2, 0, 2), ("arrive", 3, 0), ("v2", 0), ("y2", 0, 1), ("z", 1, 0, 3), ("y1", 1, 0),
    ("z", 1, 1, 3), ("v1", 1), ("y1", 1, 1), ("arrive", 3, 1), ("kv", 3, 0), ("z", 3, 0, 1), ("prev", 3, 0),
    ("z", 2, 1, 2), ("arrive", 3, 2), ("z", 2, 0, 3), ("y1", 2, 0), ("y2", 1, 0), ("z", 3, 0, 2), ("arrive", 3, 3),
    ("kv", 3, 1), ("x1", 0, 0), ("x1", 0, 1), ("z", 3, 1, 1), ("v2", 1), ("prev", 3, 1), ("q", 3), ("y2", 1, 1),
    ("z", 2, 1, 3), ("v1", 2), ("y1", 2, 1), ("v3", 0), ("y2", 2, 0), ("z", 3, 0, 3), ("y1", 3, 0), ("z", 3, 1, 2),
    ("x1", 1, 0), ("vz", 0, 2), ("x1", 1, 1), ("v3", 1), ("v2", 2), ("z", 3, 1, 3), ("v1", 3), ("y1", 3, 1),
    ("y2", 2, 1), ("vz", 0, 3), ("stage", 0), ("head", 0, 0), ("x1", 2, 0), ("vz", 1, 2), ("y2", 3, 0),
    ("head", 0, 1), ("v3", 2), ("v2", 3), ("y2", 3, 1), ("vz", 1, 3), ("stage", 1), ("head", 1, 0), ("x1", 2, 1),
    ("v3", 3), ("vz", 2, 2), ("head", 1, 1), ("x1", 3, 0), ("vz", 3, 2), ("x1", 3, 1), ("vz", 2, 3), ("stage", 2),
    ("head", 2, 0), ("head", 2, 1), ("vz", 3, 3), ("stage", 3), ("head", 3, 0), ("head", 3, 1),
]


def rope_constants():
    inverse = 500000.0 ** (-np.arange(0, HW, 2, dtype=np.float64) / HW)
    inverse = np.concatenate([inverse, inverse]).astype(np.float32).astype(np.float64)[None, :]
    near = np.arange(ROWS, dtype=np.float64)[:, None] * inverse
    far = np.arange(LINE, dtype=np.float64)[:, None] * ROWS * inverse
    return [jnp.asarray(f(angle), jnp.float32) for angle in (near, far) for f in (np.cos, np.sin)]


def take(refs, *counts):
    refs = list(refs)
    out = []
    for count in counts:
        out.append(refs[:count] if count > 1 else refs[0])
        del refs[:count]
    return out


def guarded(condition, act):
    if condition is None:
        act()
    else:
        pl.when(condition)(act)


class Copy:
    def __init__(self, log, src, dst, send, recv, device, sends=None, takes=None):
        self.log, self.parts = log, (src, dst, send, recv, device)
        self.sends, self.takes = sends, takes
        self.landed = False

    def make(self):
        src, dst, send, recv, device = self.parts
        return pltpu.make_async_remote_copy(
            src_ref=src, dst_ref=dst, send_sem=send, recv_sem=recv, device_id=device, device_id_type=MESH
        )

    def start(self):
        guarded(self.sends, lambda: self.make().start())
        self.log.append(self)

    def land(self):
        guarded(self.takes, lambda: self.make().wait_recv())
        self.landed = True

    def sent(self):
        guarded(self.sends, lambda: self.make().wait_send())


def kernel(plan, vert_ref, slash_ref, tok_hbm, gain_ref, wq_hbm, wk_hbm, wv_hbm, near_cos, near_sin, far_cos, far_sin, out_ref, *scratch):
    (
        tok, normed, w, kv, prev, ya, yb, xc, vy, vx, vz, qb, kall, vall, ob, cos_ref, sin_ref,
        local_sem, t_send, t_recv, f_send, p_send, p_recv, z_send, z_recv, y_send, y_recv,
        x_send, x_recv, vy_send, vy_recv, vx_send, vx_recv, vz_send, vz_recv, o_send, o_recv,
    ) = take(scratch, 4, 4, 1, 8, 8, 8, 8, 8, 4, 4, 4, 4, 1, 1, 4, 1, 1, *([1] * 20))
    s = lax.axis_index("seq")
    g = lax.axis_index("doc")
    core = lax.rem(g, 2)
    z = lax.rem(s, RING)
    row = s // RING
    y = lax.rem(row, COLS)
    x = row // COLS
    across = lax.rem(g - core + 2, 4)
    docs = [g, g + 1 - 2 * core, across, across + 1]

    def at(seq, doc):
        return {"seq": seq, "doc": doc}

    z_up = at(s - z + lax.rem(z + 1, RING), g)
    z_down = at(s - z + lax.rem(z + RING - 1, RING), g)
    z_up_two = at(s - z + lax.rem(z + 2, RING), g)
    z_down_two = at(s - z + lax.rem(z + RING - 2, RING), g)
    y_up = at(s - y * RING + lax.rem(y + 1, COLS) * RING, g)
    y_far = at(s - y * RING + lax.rem(y + 2, COLS) * RING, g)
    y_down = at(s - y * RING + lax.rem(y + 3, COLS) * RING, g)
    x_far = at(lax.rem(s + LINE // 2, LINE), g)
    after = at(lax.rem(s + 1, LINE), g)
    before = at(lax.rem(s + LINE - 1, LINE), g)
    mates = [at(s, doc) for doc in docs]
    peer = at(s, across + core)

    log = []

    def remote(*parts, **ends):
        return Copy(log, *parts, **ends)

    loads = [
        pltpu.make_async_copy(tok_hbm, tok[0], local_sem.at[0]),
        pltpu.make_async_copy(wk_hbm, w.at[:, 0:HW], local_sem.at[1]),
        pltpu.make_async_copy(wv_hbm, w.at[:, HW : 2 * HW], local_sem.at[2]),
        pltpu.make_async_copy(wq_hbm, w.at[:, 2 * HW :], local_sem.at[3]),
    ]
    for load in loads:
        load.start()

    barrier = pltpu.get_barrier_semaphore()
    greeted = mates[1:] + [z_up, z_down, z_up_two, z_down_two, y_up, y_far, y_down, x_far, after, before]
    for device in greeted:
        pl.semaphore_signal(barrier, inc=1, device_id=device, device_id_type=MESH)
    pl.semaphore_wait(barrier, len(greeted))

    even, odd = core == 0, core == 1
    lower, upper = x == 0, x == 1
    gives_prev = jnp.logical_and(z == RING - 1, s < LINE - 1)
    takes_prev = jnp.logical_and(z == 0, s > 0)

    def rows_of(c):
        return pl.ds(c * PART, PART)

    def chunk_sem(k, c):
        return t_recv.at[(k - 2) * CHUNKS + c]

    crossing = [
        [
            remote(
                tok_hbm.at[rows_of(c)], tok[k].at[rows_of(c)], t_send.at[c], chunk_sem(k, c), peer,
                sends=even if k == 2 else odd,
            )
            for c in range(CHUNKS)
        ]
        for k in (2, 3)
    ]
    handed = [
        [
            remote(
                tok[k].at[rows_of(c)], tok[k].at[rows_of(c)], f_send.at[c], chunk_sem(k, c), mates[1],
                sends=even if k == 2 else odd,
            )
            for c in range(CHUNKS)
        ]
        for k in (2, 3)
    ]
    beside = remote(tok_hbm, tok[1], t_send.at[CHUNKS], t_recv.at[2 * CHUNKS], mates[1])

    def norm(k, start, count):
        def body(i, carry):
            at_rows = pl.ds(pl.multiple_of(start + i * 16, 16), 16)
            wide = tok[k][at_rows, :].astype(jnp.float32)
            scale = lax.rsqrt(jnp.sum(wide * wide, axis=-1, keepdims=True) * (1.0 / WIDTH) + 1e-05)
            normed[k][at_rows, :] = (wide * scale * gain_ref[...]).astype(jnp.bfloat16)
            return carry

        lax.fori_loop(0, count // 16, body, 0)

    def do_own(k):
        turn_cos, turn_sin = far_cos[pl.ds(s, 1), :], far_sin[pl.ds(s, 1), :]
        sign = jnp.where(lax.broadcasted_iota(jnp.int32, (1, HW), 1) < HW // 2, -1.0, 1.0)
        cos_ref[...] = near_cos[...] * turn_cos - near_sin[...] * turn_sin
        sin_ref[...] = (near_sin[...] * turn_cos + near_cos[...] * turn_sin) * sign
        loads[0].wait()
        norm(0, 0, ROWS)

    def do_beside(k):
        beside.land()
        norm(1, 0, ROWS)

    def do_arrive(k, c):
        crossing[k - 2][c].land()
        handed[k - 2][c].start()
        handed[k - 2][c].landed = True
        if k == 2 and c == CHUNKS - 3:
            for copy in crossing[1]:
                copy.start()
        norm(k, c * PART, PART)

    def rotate(value, at_rows):
        return value * cos_ref[at_rows, :] + pltpu.roll(value, HW // 2, 1) * sin_ref[at_rows, :]

    ready = set()

    def loaded(*which):
        for i in which:
            if i not in ready:
                loads[i].wait()
                ready.add(i)

    def do_kv(k, h):
        loaded(1, 2)
        u = 2 * k + h
        at_rows = slice(h * HALF, (h + 1) * HALF)
        both = jnp.dot(normed[k][at_rows, :], w[:, 0 : 2 * HW], preferred_element_type=jnp.float32)
        kv[u][z, :, 0:HW] = rotate(both[:, 0:HW], at_rows).astype(jnp.bfloat16)
        kv[u][z, :, HW:] = both[:, HW:].astype(jnp.bfloat16)

    def do_q(k):
        loaded(3)
        wide = jnp.dot(normed[k][...], w[:, 2 * HW :], preferred_element_type=jnp.float32)
        for h in range(HEADS):
            qb[k][h * ROWS : (h + 1) * ROWS, :] = rotate(wide[:, h * HW : (h + 1) * HW], slice(0, ROWS)).astype(jnp.bfloat16)

    def ring(buf, k, send, recv):
        behind, ahead = lax.rem(z + RING - 2, RING), lax.rem(z + 2, RING)
        routes = [(z, z_up_two), (z, z_down_two), (z, z_up), (z, z_down)]
        routes += [(behind, z_up_two) if k % 2 == 0 else (ahead, z_down_two), (behind, z_up), (ahead, z_down)]
        return [
            remote(buf.at[place], buf.at[place], send.at[k * 7 + i], recv.at[k * 7 + i], device)
            for i, (place, device) in enumerate(routes)
        ]

    z_hops = [ring(kv[u], u, z_send, z_recv) for u in range(UNITS)]
    vz_hops = [ring(vz[k], k, vz_send, vz_recv) for k in range(DOCS)]

    def step(hops, j):
        lands = ((), (0, 1), (2, 3, 4, 5, 6))[j - 1]
        starts = (range(4), range(4, 7), ())[j - 1]
        for i in lands:
            hops[i].land()
        for i in starts:
            hops[i].start()

    def do_z(k, h, j):
        step(z_hops[2 * k + h], j)

    def do_vz(k, j):
        step(vz_hops[k], j)

    prevs = [
        remote(kv[u].at[z], prev[u], p_send.at[u], p_recv.at[u], after, sends=gives_prev, takes=takes_prev)
        for u in range(UNITS)
    ]

    def do_prev(k, h):
        prevs[2 * k + h].start()

    offset = [[slash_ref[docs[k], g, t] for t in range(SLOTS)] for k in range(DOCS)]
    vertical = [[vert_ref[docs[k], g, i] for i in range(4)] for k in range(DOCS)]
    mine = [vert_ref[docs[k], g, lax.rem(z, 4)] for k in range(DOCS)]
    shift = [[(offset[k][t] - z + RING - 1) // RING for t in range(SLOTS)] for k in range(DOCS)]

    def turns(k, t):
        steps = lax.rem(shift[k][t], COLS)
        return steps if t < 2 else lax.rem(COLS - steps, COLS)

    y_near = [
        [
            remote(ya[u].at[0, 0:2], ya[u].at[1, 0:2], y_send.at[u * 3], y_recv.at[u * 3], y_up),
            remote(ya[u].at[0, 2:4], ya[u].at[1, 2:4], y_send.at[u * 3 + 1], y_recv.at[u * 3 + 1], y_down),
        ]
        for u in range(UNITS)
    ]
    y_over = [
        remote(yb[u].at[0], yb[u].at[1], y_send.at[u * 3 + 2], y_recv.at[u * 3 + 2], y_far) for u in range(UNITS)
    ]
    x_over = [
        remote(xc[u].at[0], xc[u].at[1], x_send.at[u], x_recv.at[u], x_far, sends=lower, takes=upper)
        for u in range(UNITS)
    ]
    vy_over = [
        [
            remote(vy[k].at[y], vy[k].at[y], vy_send.at[k * 3 + i], vy_recv.at[k * 3 + i], device)
            for i, device in enumerate((y_up, y_far, y_down))
        ]
        for k in range(DOCS)
    ]
    vx_over = [
        remote(vx[k].at[0], vx[k].at[1], vx_send.at[k], vx_recv.at[k], x_far, sends=lower, takes=upper)
        for k in range(DOCS)
    ]

    def do_y1(k, h):
        u = 2 * k + h
        for t in range(SLOTS):
            ya[u][0, t] = kv[u][lax.rem(z - offset[k][t] + LINE, RING)]
        for copy in y_near[u]:
            copy.start()

    def do_y2(k, h):
        u = 2 * k + h
        for copy in y_near[u]:
            copy.land()
        for t in range(SLOTS):
            yb[u][0, t] = ya[u][lax.rem(turns(k, t), 2), t]
        y_over[u].start()

    def do_x1(k, h):
        u = 2 * k + h
        y_over[u].land()
        for t in range(SLOTS):
            xc[u][0, t] = yb[u][turns(k, t) // 2, t]
        x_over[u].start()

    def do_v1(k):
        for h in range(2):

            @pl.when(z // 4 == h)
            def _():
                vy[k][y] = kv[2 * k + h][lax.rem(mine[k], RING)]

        for copy in vy_over[k]:
            copy.start()

    def do_v2(k):
        for copy in vy_over[k]:
            copy.land()
        vx[k][0] = vy[k][lax.rem(mine[k] // RING, COLS)]
        vx_over[k].start()

    def do_v3(k):
        vx_over[k].land()
        vz[k][z] = vx[k][x * (mine[k] < LINE // 2).astype(jnp.int32)]
        do_vz(k, 1)

    def columns(i):
        return pl.ds(pl.multiple_of(g * 512 + i * HW, HW), HW)

    out_own = [
        pltpu.make_async_copy(ob[0].at[i], out_ref.at[:, columns(i)], local_sem.at[4 + i]) for i in range(HEADS)
    ]

    def out_copy(k, i, receive):
        return remote(
            ob[k].at[i], out_ref.at[:, columns(i)], o_send.at[(k - 1) * HEADS + i], o_recv.at[receive * HEADS + i],
            mates[k],
        )

    out_sent = [None] + [[out_copy(k, i, 0 if k == 1 else 1 + core) for i in range(HEADS)] for k in range(1, DOCS)]
    out_got = [out_copy(1, i, source) for source in range(3) for i in range(HEADS)]

    low = jnp.float32(-jnp.inf)

    bias = {}

    def do_stage(k):
        for h in range(2):
            u = 2 * k + h
            prevs[u].land()
            x_over[u].land()

            def put(i, value):
                at_rows = slice(i * ROWS + h * HALF, i * ROWS + (h + 1) * HALF)
                kall[at_rows, :] = value[:, 0:HW]
                vall[at_rows, :] = value[:, HW:]

            put(0, kv[u][z])

            @pl.when(z > 0)
            def _():
                put(1, kv[u][lax.rem(z + RING - 1, RING)])

            @pl.when(takes_prev)
            def _():
                put(1, prev[u][...])

            @pl.when(s == 0)
            def _():
                put(1, jnp.zeros((HALF, 2 * HW), jnp.bfloat16))

            for t in range(SLOTS):
                put(2 + t, xc[u][x * (shift[k][t] > y).astype(jnp.int32), t])
            for i in range(4):
                put(2 + SLOTS + i, vz[k][i + 4 * h])
        allowed = [s >= 1] + [s >= offset[k][t] for t in range(SLOTS)]
        for i in range(4):
            good = vertical[k][i] < s - 1
            for t in range(SLOTS):
                good = jnp.logical_and(good, vertical[k][i] != s - offset[k][t])
            allowed.append(good)
        bias[k] = [jnp.where(good, jnp.float32(0.0), low) for good in allowed]

    def do_head(k, pair):
        blocks = 2 + SLOTS + 4
        causal = lax.broadcasted_iota(jnp.int32, (ROWS, ROWS), 1) <= lax.broadcasted_iota(jnp.int32, (ROWS, ROWS), 0)
        for i in (2 * pair, 2 * pair + 1):
            scores = lax.dot_general(
                qb[k][i * ROWS : (i + 1) * ROWS, :],
                kall[...],
                (((1,), (1,)), ((), ())),
                preferred_element_type=jnp.float32,
            )
            tiles = [scores[:, n * ROWS : (n + 1) * ROWS] for n in range(blocks)]
            tiles = [jnp.where(causal, tiles[0], low)] + [tiles[n] + bias[k][n - 1] for n in range(1, blocks)]
            highest = tiles[0]
            for tile in tiles[1:]:
                highest = jnp.maximum(highest, tile)
            highest = jnp.max(highest, axis=1, keepdims=True)
            raised = [jnp.exp2((tile - highest) * (HW ** (-0.5) * 1.4426950408889634)) for tile in tiles]
            total = raised[0]
            for tile in raised[1:]:
                total = total + tile
            total = jnp.sum(total, axis=1, keepdims=True)
            weights = jnp.concatenate([tile.astype(jnp.bfloat16) for tile in raised], axis=1)
            mixed = jnp.dot(weights, vall[...], preferred_element_type=jnp.float32) / total
            ob[k][i] = mixed.astype(jnp.bfloat16)
            if k == 0:
                out_own[i].start()
            else:
                out_sent[k][i].start()
                out_sent[k][i].landed = True

    for copy in crossing[0]:
        copy.start()
    beside.start()
    does = {
        "own": do_own, "beside": do_beside, "arrive": do_arrive, "kv": do_kv, "q": do_q, "z": do_z, "vz": do_vz,
        "prev": do_prev, "y1": do_y1, "y2": do_y2, "x1": do_x1, "v1": do_v1, "v2": do_v2, "v3": do_v3,
        "stage": do_stage, "head": do_head,
    }
    for name, *which in plan:
        does[name](*which)

    loaded(1, 2, 3)
    for copy in log:
        if not copy.landed:
            copy.land()
        copy.sent()
    for copy in out_own:
        copy.wait()
    for copy in out_got:
        copy.land()


def layer(plan, collective_id, tokens, norm_gain, w_query, key_weight, value_weight, vertical_blocks, slash_offsets):
    bf16 = jnp.bfloat16
    unit = (HALF, 2 * HW)
    dma = pltpu.SemaphoreType.DMA

    def many(shape):
        return [pltpu.VMEM(shape, bf16)] * DOCS

    scratch = (
        many((ROWS, WIDTH))
        + many((ROWS, WIDTH))
        + [pltpu.VMEM((WIDTH, 6 * HW), bf16)]
        + many((RING,) + unit) * 2
        + many(unit) * 2
        + many((2, SLOTS) + unit) * 6
        + many((COLS,) + unit)
        + many((2,) + unit)
        + many((RING,) + unit)
        + many((HEADS * ROWS, HW))
        + [pltpu.VMEM((10 * ROWS, HW), bf16)] * 2
        + many((HEADS, ROWS, HW))
        + [pltpu.VMEM((ROWS, HW), jnp.float32)] * 2
        + [dma((4 + HEADS,)), dma((CHUNKS + 1,)), dma((2 * CHUNKS + 1,)), dma((CHUNKS,))]
    )
    for count in (8, 56, 24, 8, 12, 4, 28, 12):
        scratch += [dma((count,))] * 2
    smem = pl.BlockSpec(memory_space=pltpu.SMEM)
    vmem = pl.BlockSpec(memory_space=pltpu.VMEM)
    hbm = pl.BlockSpec(memory_space=pl.ANY)
    out = pl.pallas_call(
        functools.partial(kernel, plan),
        out_shape=pltpu.VMEM((ROWS, DOCS * HEADS * HW), bf16),
        in_specs=[smem, smem, hbm, vmem, hbm, hbm, hbm] + [vmem] * 4,
        out_specs=vmem,
        scratch_shapes=scratch,
        compiler_params=pltpu.CompilerParams(
            collective_id=collective_id, has_side_effects=True, vmem_limit_bytes=60 * 1024 * 1024
        ),
    )(
        vertical_blocks,
        slash_offsets,
        tokens[0],
        norm_gain[None, :],
        w_query,
        key_weight,
        value_weight,
        *rope_constants(),
    )
    return out[None]


IN_SPECS = (
    P("doc", "seq", None),
    P(),
    P(None, "doc"),
    P(None, "doc"),
    P(None, "doc"),
    P(),
    P(),
)


def solution(mesh):
    return jax.shard_map(
        functools.partial(layer, PLAN, 0),
        mesh=mesh,
        in_specs=IN_SPECS,
        out_specs=P("doc", "seq", None),
        check_vma=False,
    )
```
